128 devices in a mesh: dp: 8 (over x, core), ctx: 4 (over y), tensor: 4 (over z).
Axes of the slice: x: 4, y: 4, z: 4, core: 2. Of those that a mesh axis runs over, the one named last changes fastest.
Arguments:
- hidden: bfloat16 [8, 16384, 2560], P('dp', 'ctx', 'tensor'), may hold values from -6 to 6
- depth: int32 [8, 16384], P('dp', 'ctx'), may hold values from 1 to 4, as said below
- qkv_weight: bfloat16 [2560, 3, 2560], P(None, None, 'tensor'), may hold values from -0.125 to 0.125
- out_weight: bfloat16 [2560, 2560], P('tensor'), may hold values from -0.125 to 0.125
Outputs:
- update: bfloat16 [8, 16384, 2560], P('dp', 'ctx', 'tensor')
The draws below stay inside these ranges and needn't reach their ends.
Inputs may be any that keep to these rules, and one draw needn't show every extreme that they name: In every aligned block of 4096 positions of a document at most 1024 tokens have depth at least 3, and some block has exactly 1024; over all documents exactly 16384 tokens do.
All inputs are finite; a program needn't handle non-finite values.
Results may differ from the reference program's by a relative error of at most 0.012.
The reference program's roundings to bfloat16 on the way count: a program that leaves them out, or rounds other values in their place, can miss the bound.
Values may be sent and summed in bfloat16 or wider, within the bound.
No kernel may reach another device: no remote copies, remote signals or barrier semaphores. Data moves between devices by JAX's collectives and lax.ppermute only.
A program may use at most 256 MiB of HBM per device.

```python
import jax
import jax.numpy as jnp
from jax import lax

D = 2560
HEADS = 20
HD = 128
RECURSION = 3
MAX_DEPTH = 4
TOK_DEV = 4096
ACT_DEV = 512
CAP = 1024
DOCS = 8
LEN = 16384
N_DP = 8
N_CTX = 4
N_TENSOR = 4


def draw_depth(key, part):
    shard_total = DOCS * (LEN // TOK_DEV)
    half_total = shard_total // 2
    key_order, key_load, key_place, key_deep, key_shallow = jax.random.split(jax.random.fold_in(key, 17), 5)
    loads = jax.random.randint(key_load, (half_total,), 0, CAP + 1)
    loads = loads.at[0].set(CAP)
    paired = jnp.concatenate([loads, CAP - loads])
    shuffled = jax.random.permutation(key_order, shard_total)
    shard_counts = jnp.zeros((shard_total,), jnp.int32).at[shuffled].set(paired.astype(jnp.int32))
    place_keys = jax.random.split(key_place, shard_total)
    ranking = jax.vmap(lambda single: jax.random.permutation(single, TOK_DEV))(place_keys)
    chosen = ranking < shard_counts[:, None]
    deeper = jax.random.randint(key_deep, (shard_total, TOK_DEV), RECURSION, MAX_DEPTH + 1)
    shallow = jax.random.randint(key_shallow, (shard_total, TOK_DEV), 1, RECURSION)
    return jnp.where(chosen, deeper, shallow).reshape(DOCS, LEN).astype(jnp.int32)


def levels(rng, shape, cuts, low, largest):
    def one(axis_at, parts):
        draws = jax.random.uniform(jax.random.fold_in(jax.random.fold_in(rng, 6), axis_at), (parts,), jnp.float32, low / len(cuts), largest / len(cuts))
        return jnp.repeat(jnp.exp(draws), shape[axis_at] // parts).reshape((-1,) + (1,) * (len(shape) - axis_at - 1))

    factor_of = one(*cuts[0])
    for cut in cuts[1:]:
        factor_of = factor_of * one(*cut)
    return factor_of


def bell_draw(stream_key, shape, scale, limit, pieces=(), kind=jnp.bfloat16):
    array = scale * jax.random.normal(stream_key, shape, jnp.float32)
    if pieces:
        array = array * levels(stream_key, shape, pieces, -0.22, 0.18)
    return jnp.clip(array, -limit, limit).astype(kind)


def setup_inputs(seed: int = 0) -> dict:
    streams_of = jax.random.split(jax.random.key(seed), 5)
    return {
        "hidden": bell_draw(streams_of[0], (DOCS, LEN, D), 1.0, 6.0, ((0, 8), (1, 4), (2, 4))),
        "depth": draw_depth(jax.random.fold_in(streams_of[4], 71), 0),
        "qkv_weight": bell_draw(streams_of[2], (D, 3, HEADS * HD), D ** -0.5, 0.125, ((2, 4),)),
        "out_weight": bell_draw(streams_of[3], (HEADS * HD, D), (HEADS * HD) ** -0.5, 0.125, ((0, 4),)),
    }


score_scale = 0.25
norm_epsilon = 1e-05
head_epsilon = 1e-06

def head_normed(values):
    row_count = values.shape[0]
    per_head = values.reshape(row_count, -1, HD)
    factor = lax.rsqrt(lax.optimization_barrier(jnp.mean(per_head * per_head, axis=2, keepdims=True)) + head_epsilon)
    return (per_head * factor).reshape(row_count, -1).astype(jnp.bfloat16)

def reference(hidden, depth, qkv_weight, out_weight):
    doc_total, length, feature_width = hidden.shape
    head_width = qkv_weight.shape[2]
    active_total = ACT_DEV * N_DP * N_CTX
    doc_room = min(length, N_CTX * CAP)
    active = depth >= RECURSION
    doc_counts = lax.optimization_barrier(jnp.sum(active.astype(jnp.int32), axis=1)).astype(jnp.int32)
    doc_starts = (jnp.cumsum(doc_counts) - doc_counts).astype(jnp.int32)
    flat_index = jnp.nonzero(active.reshape(-1), size=active_total, fill_value=0)[0].astype(jnp.int32)
    token_rows = hidden.reshape(-1, feature_width)[flat_index].astype(jnp.float32)
    factor = lax.rsqrt(lax.optimization_barrier(jnp.mean(token_rows * token_rows, axis=1, keepdims=True)) + norm_epsilon)
    normed = (token_rows * factor).astype(jnp.bfloat16)
    projection = jnp.dot(normed, qkv_weight.reshape(feature_width, 3 * head_width), preferred_element_type=jnp.float32)
    queries = head_normed(projection[:, :head_width])
    key_rows = head_normed(projection[:, head_width:2 * head_width])
    value_rows = projection[:, 2 * head_width:].astype(jnp.bfloat16)
    positions = (flat_index % length).astype(jnp.int32)
    doc_of = (flat_index // length).astype(jnp.int32)
    padding = jnp.zeros((doc_room, head_width), jnp.bfloat16)
    padded_queries = jnp.concatenate([queries, padding], axis=0)
    padded_keys = jnp.concatenate([key_rows, padding], axis=0)
    padded_values = jnp.concatenate([value_rows, padding], axis=0)
    padded_positions = jnp.concatenate([positions, jnp.zeros((doc_room,), jnp.int32)], axis=0)

    def one_document(doc_number):
        doc_begin = doc_starts[doc_number]
        query_block = lax.dynamic_slice_in_dim(padded_queries, doc_begin, doc_room).astype(jnp.float32).reshape(doc_room, -1, HD)
        key_block = lax.dynamic_slice_in_dim(padded_keys, doc_begin, doc_room).astype(jnp.float32).reshape(doc_room, -1, HD)
        value_block = lax.dynamic_slice_in_dim(padded_values, doc_begin, doc_room).astype(jnp.float32).reshape(doc_room, -1, HD)
        position_block = lax.dynamic_slice_in_dim(padded_positions, doc_begin, doc_room)
        filled = jnp.arange(doc_room, dtype=jnp.int32) < doc_counts[doc_number]
        allowed = filled[:, None] & filled[None, :] & (position_block[None, :] <= position_block[:, None])
        scores = jnp.einsum('qhd,khd->hqk', query_block, key_block) * score_scale
        weights = jnp.where(allowed[None], jnp.exp(scores), 0.0)
        rounded = lax.optimization_barrier(weights.astype(jnp.bfloat16)).astype(jnp.float32)
        numerator = jnp.einsum('hqk,khd->qhd', rounded, value_block)
        denominator = lax.optimization_barrier(jnp.sum(weights, axis=2)) + (1.0 - filled.astype(jnp.float32))[None, :]
        context = numerator / jnp.transpose(denominator)[:, :, None]
        return context.reshape(doc_room, head_width).astype(jnp.bfloat16)
    contexts = lax.map(one_document, jnp.arange(doc_total, dtype=jnp.int32))
    within = (jnp.arange(active_total, dtype=jnp.int32) - doc_starts[doc_of]).astype(jnp.int32)
    context_rows = contexts[doc_of, within]
    group_width = head_width // N_TENSOR
    summed = jnp.zeros((active_total, feature_width), jnp.float32)
    for group_index in range(N_TENSOR):
        lower = group_index * group_width
        partial_value = jnp.dot(context_rows[:, lower:lower + group_width], out_weight[lower:lower + group_width], preferred_element_type=jnp.float32).astype(jnp.bfloat16)
        summed = summed + lax.optimization_barrier(partial_value).astype(jnp.float32)
    update = jnp.zeros((doc_total * length, feature_width), jnp.bfloat16).at[flat_index].set(summed.astype(jnp.bfloat16))
    return update.reshape(doc_total, length, feature_width)
```

```python
import math

import jax
import jax.numpy as jnp
from jax import lax
from jax.experimental import pallas as pl
from jax.experimental.pallas import tpu as pltpu
from jax.sharding import PartitionSpec as P

HD = 128
RECURSION = 3
CAP = 1024
HALF = CAP // 2
SUB = CAP // 4
TOK_BLOCK = 256
WINDOW = 384
ROOM = CAP + WINDOW

score_scale = 0.25
norm_epsilon = 1e-05
head_epsilon = 1e-06
EXP2_SCALE = score_scale / math.log(2.0)
VMEM_LIMIT = 56 * 1024 * 1024

bf16 = jnp.bfloat16
f32 = jnp.float32


def params(**more):
    return pltpu.CompilerParams(vmem_limit_bytes=VMEM_LIMIT, **more)


def slot_onehot(depth_row, shift):
    active = depth_row >= RECURSION
    flags = jnp.broadcast_to(jnp.where(active, 1.0, 0.0), (8, TOK_BLOCK)).astype(bf16)
    before = lax.broadcasted_iota(jnp.int32, (TOK_BLOCK, TOK_BLOCK), 0)
    after = lax.broadcasted_iota(jnp.int32, (TOK_BLOCK, TOK_BLOCK), 1)
    earlier = jnp.where(before < after, 1.0, 0.0).astype(bf16)
    rank = jnp.dot(flags, earlier, preferred_element_type=f32)[0:1].astype(jnp.int32)
    slot = jnp.where(active, rank + shift, -1)
    rows = lax.broadcasted_iota(jnp.int32, (WINDOW, TOK_BLOCK), 0)
    return jnp.where(rows == slot, 1.0, 0.0).astype(bf16)


def window_start(offset):
    return pl.multiple_of((offset >> 7) << 7, 128)


def compact_kernel(offs_ref, depth_ref, tok_ref, o0, o1, o2, o3, buf):
    step = pl.program_id(0)

    @pl.when(step == 0)
    def _():
        buf[...] = jnp.zeros_like(buf)

    for sub in range(2):
        offset = offs_ref[step * 2 + sub]
        start = window_start(offset)
        onehot = slot_onehot(depth_ref[sub], offset - start)
        picked = jnp.dot(
            onehot,
            tok_ref[sub * TOK_BLOCK : (sub + 1) * TOK_BLOCK, :],
            preferred_element_type=f32,
        ).astype(bf16)
        buf[pl.ds(start, WINDOW), :] = buf[pl.ds(start, WINDOW), :] + picked

    @pl.when(step == pl.num_programs(0) - 1)
    def _():
        for i, o in enumerate((o0, o1, o2, o3)):
            o[...] = buf[i * SUB : (i + 1) * SUB, :]


def compact_rows(tokens, depth_blocks, offsets):
    length, width = tokens.shape
    steps = length // (2 * TOK_BLOCK)
    sub = jax.ShapeDtypeStruct((SUB, width), bf16)
    return pl.pallas_call(
        compact_kernel,
        out_shape=(sub,) * 4,
        grid_spec=pltpu.PrefetchScalarGridSpec(
            num_scalar_prefetch=1,
            grid=(steps,),
            in_specs=[
                pl.BlockSpec((2, 1, TOK_BLOCK), lambda i, o: (i, 0, 0)),
                pl.BlockSpec((2 * TOK_BLOCK, width), lambda i, o: (i, 0)),
            ],
            out_specs=(pl.BlockSpec((SUB, width), lambda i, o: (0, 0)),) * 4,
            scratch_shapes=[pltpu.VMEM((ROOM, width), bf16)],
        ),
        compiler_params=params(),
        name="compact",
    )(offsets, depth_blocks, tokens)


def project_kernel(
    place, x0, x1, a0, a1, b0, b1, c0, d1, w_ref, o0, o1, o2, o3, q4, kv4, xs, acc
):
    part = pl.program_id(0)
    t = place[0]
    ctx = place[1]
    width = x0.shape[1]

    @pl.when(part == 0)
    def _():
        for sub, pieces in enumerate(((x0, a0, b0, c0), (x1, a1, b1, d1))):
            squares = jnp.zeros((SUB, 1), f32)
            for piece in pieces:
                wide = piece[...].astype(f32)
                squares = squares + jnp.sum(wide * wide, axis=1, keepdims=True)
            factor = lax.rsqrt(squares * (1.0 / (4 * width)) + norm_epsilon)
            for shift, piece in zip((0, 3, 1, 2), pieces):
                lane = pl.multiple_of(((t + shift) & 3) * width, 128)
                normed = (piece[...].astype(f32) * factor).astype(bf16)
                xs[sub * SUB : (sub + 1) * SUB, pl.ds(lane, width)] = normed

    acc[...] = jnp.dot(xs[...], w_ref[...], preferred_element_type=f32)
    for slot, out in enumerate((o0, o1, o2, o3, None)):
        if out is None:
            y = acc[:, 4 * HD : 5 * HD]
        else:
            y = acc[:, pl.ds(pl.multiple_of(((ctx + slot) & 3) * HD, HD), HD)]
        scale = lax.rsqrt(jnp.mean(y * y, axis=1, keepdims=True) + head_epsilon)
        z = (y * jnp.where(part == 2, 1.0, scale)).astype(bf16)
        if out is None:

            @pl.when(part == 0)
            def _():
                q4[...] = z

            @pl.when(part > 0)
            def _():
                kv4[0] = z

        else:
            out[0] = z


def project(place, own, left, right, far, weight):
    width = own[0].shape[1]
    model = 4 * width
    sub = pl.BlockSpec((SUB, width), lambda j, p: (0, 0))
    stacked = jax.ShapeDtypeStruct((3, HALF, HD), bf16)
    stacked_spec = pl.BlockSpec((1, HALF, HD), lambda j, p: (j, 0, 0))
    return pl.pallas_call(
        project_kernel,
        out_shape=(stacked,) * 4
        + (
            jax.ShapeDtypeStruct((HALF, HD), bf16),
            jax.ShapeDtypeStruct((2, HALF, HD), bf16),
        ),
        grid_spec=pltpu.PrefetchScalarGridSpec(
            num_scalar_prefetch=1,
            grid=(3,),
            in_specs=[sub] * 8 + [pl.BlockSpec((model, 5 * HD), lambda j, p: (0, j))],
            out_specs=(stacked_spec,) * 4
            + (
                pl.BlockSpec((HALF, HD), lambda j, p: (0, 0)),
                pl.BlockSpec((1, HALF, HD), lambda j, p: (jnp.maximum(j - 1, 0), 0, 0)),
            ),
            scratch_shapes=[
                pltpu.VMEM((HALF, model), bf16),
                pltpu.VMEM((HALF, 5 * HD), f32),
            ],
        ),
        compiler_params=params(),
        name="project",
    )(place, *own, *left, *right, *far, weight)


def attend_chunk(chunk, query, count_of, ks, vs, acc):
    def add_tile(key_chunk, masked):
        scores = lax.dot_general(
            query, ks[key_chunk], (((1,), (1,)), ((), ())), preferred_element_type=f32
        )
        weights = jnp.exp2(scores * EXP2_SCALE)
        if masked:
            row = lax.broadcasted_iota(jnp.int32, (HALF, HALF), 0)
            col = lax.broadcasted_iota(jnp.int32, (HALF, HALF), 1)
            weights = jnp.where(col <= row, weights, 0.0)
        acc[...] += jnp.dot(weights.astype(bf16), vs[key_chunk], preferred_element_type=f32)

    acc[...] = jnp.zeros_like(acc)

    def body(key_chunk, carry):
        @pl.when(count_of(key_chunk >> 1) > (key_chunk & 1) * HALF)
        def _():
            add_tile(key_chunk, False)

        return carry

    lax.fori_loop(0, chunk, body, 0)
    add_tile(chunk, True)
    total = acc[:, HD:]
    return (acc[:, :HD] / jnp.where(total == 0.0, 1.0, total)).astype(bf16)


def value_rows(value, half, count):
    rows = lax.broadcasted_iota(jnp.int32, (HALF, HD), 0) + half * HALF
    return value, jnp.where(rows < count, 1.0, 0.0).astype(bf16)


def attend_main_kernel(place, *refs):
    inputs, outs, (qs, ks, vs, cs, acc) = refs[:8], refs[8:16], refs[16:]
    ctx = place[0]

    def count_of(block):
        return place[1 + ((ctx - block) & 3)]

    for s in range(4):
        block = (ctx - s) & 3
        for half in range(2):
            chunk = block * 2 + half
            source = inputs[2 * s + half]
            qs[chunk] = source[0]
            ks[chunk] = source[1]
            value, flag = value_rows(source[2], half, place[1 + s])
            vs[chunk, :, :HD] = value
            vs[chunk, :, HD:] = flag

    def body(chunk, carry):
        filled = count_of(chunk >> 1) > (chunk & 1) * HALF

        @pl.when(filled)
        def _():
            cs[chunk] = attend_chunk(chunk, qs[chunk], count_of, ks, vs, acc)

        @pl.when(jnp.logical_not(filled))
        def _():
            cs[chunk] = jnp.zeros((HALF, HD), bf16)

        return carry

    lax.fori_loop(0, 8, body, 0)
    for s in range(4):
        for half in range(2):
            outs[2 * s + half][...] = cs[((ctx - s) & 3) * 2 + half]


def vmem_specs(count):
    return [pl.BlockSpec(memory_space=pltpu.VMEM)] * count


def attend_main(place, inputs):
    return pl.pallas_call(
        attend_main_kernel,
        out_shape=(jax.ShapeDtypeStruct((HALF, HD), bf16),) * 8,
        in_specs=[pl.BlockSpec(memory_space=pltpu.SMEM)] + vmem_specs(8),
        out_specs=tuple(vmem_specs(8)),
        scratch_shapes=[
            pltpu.VMEM((8, HALF, HD), bf16),
            pltpu.VMEM((8, HALF, HD), bf16),
            pltpu.VMEM((8, HALF, 2 * HD), bf16),
            pltpu.VMEM((8, HALF, HD), bf16),
            pltpu.VMEM((HALF, 2 * HD), f32),
        ],
        compiler_params=params(),
        name="attend_main",
    )(place, *inputs)


def attend_last_kernel(place, q0, q1, kv0, kv1, o0, o1, ks, vs, acc):
    ctx = place[0]

    def count_of(block):
        return place[1 + ((ctx - block) & 3)]

    for block in range(4):

        @pl.when(block <= ctx)
        def _():
            for half, source in enumerate((kv0, kv1)):
                chunk = block * 2 + half
                ks[chunk] = source[block, 0]
                value, flag = value_rows(source[block, 1], half, count_of(block))
                vs[chunk, :, :HD] = value
                vs[chunk, :, HD:] = flag

    for half, (query, out) in enumerate(((q0, o0), (q1, o1))):
        filled = place[1] > half * HALF

        @pl.when(filled)
        def _():
            out[...] = attend_chunk(ctx * 2 + half, query[...], count_of, ks, vs, acc)

        @pl.when(jnp.logical_not(filled))
        def _():
            out[...] = jnp.zeros((HALF, HD), bf16)


def attend_last(place, queries, gathered):
    return pl.pallas_call(
        attend_last_kernel,
        out_shape=(jax.ShapeDtypeStruct((HALF, HD), bf16),) * 2,
        in_specs=[pl.BlockSpec(memory_space=pltpu.SMEM)] + vmem_specs(4),
        out_specs=tuple(vmem_specs(2)),
        scratch_shapes=[
            pltpu.VMEM((8, HALF, HD), bf16),
            pltpu.VMEM((8, HALF, 2 * HD), bf16),
            pltpu.VMEM((HALF, 2 * HD), f32),
        ],
        compiler_params=params(),
        name="attend_last",
    )(place, *queries, *gathered)


def output_kernel(offs_ref, depth_ref, *refs):
    groups, weights, (out, cbuf, rows) = refs[:15], refs[15:19], refs[19:]
    step = pl.program_id(0)

    @pl.when(step == 0)
    def _():
        rows[CAP:, :] = jnp.zeros((WINDOW, rows.shape[1]), bf16)
        for half in range(2):
            total = None
            for source in range(4):
                first = groups[:5]
                rest = groups[5 + 5 * half : 10 + 5 * half]
                if source < 3:
                    pair, trio = first[source], rest[source]
                    last = pair[half]
                    own = pair[2 + half]
                    sixth = [trio[i] for i in range(6)]
                else:
                    last = first[3][half]
                    own = first[4][half]
                    sixth = [rest[3][i] for i in range(3)] + [rest[4][i] for i in range(3)]
                cbuf[:, 0:HD] = own
                for i in range(6):
                    lane = HD * (1 + i // 2)
                    low = (i % 2) * SUB
                    cbuf[low : low + SUB, lane : lane + HD] = sixth[i]
                cbuf[:, 4 * HD : 5 * HD] = last
                term = jnp.dot(cbuf[...], weights[source][...], preferred_element_type=f32)
                term = term.astype(bf16).astype(f32)
                total = term if total is None else total + term
            rows[half * HALF : (half + 1) * HALF, :] = total.astype(bf16)

    for sub in range(2):
        offset = offs_ref[step * 2 + sub]
        start = window_start(offset)
        onehot = slot_onehot(depth_ref[sub], offset - start)
        spread = lax.dot_general(
            onehot,
            rows[pl.ds(start, WINDOW), :],
            (((0,), (0,)), ((), ())),
            preferred_element_type=f32,
        )
        out[sub * TOK_BLOCK : (sub + 1) * TOK_BLOCK, :] = spread.astype(bf16)


def output_update(offsets, depth_blocks, groups, weights, length):
    width = weights[0].shape[1]
    steps = length // (2 * TOK_BLOCK)

    def whole(array):
        rank = array.ndim
        return pl.BlockSpec(array.shape, lambda i, o: (0,) * rank)

    return pl.pallas_call(
        output_kernel,
        out_shape=jax.ShapeDtypeStruct((length, width), bf16),
        grid_spec=pltpu.PrefetchScalarGridSpec(
            num_scalar_prefetch=1,
            grid=(steps,),
            in_specs=[pl.BlockSpec((2, 1, TOK_BLOCK), lambda i, o: (i, 0, 0))]
            + [whole(a) for a in groups]
            + [whole(a) for a in weights],
            out_specs=pl.BlockSpec((2 * TOK_BLOCK, width), lambda i, o: (i, 0)),
            scratch_shapes=[
                pltpu.VMEM((HALF, 5 * HD), bf16),
                pltpu.VMEM((ROOM, width), bf16),
            ],
        ),
        compiler_params=params(),
        name="output",
    )(offsets, depth_blocks, *groups, *weights)


def shift(value, axis, distance):
    size = lax.axis_size(axis)
    return lax.ppermute(value, axis, [(i, (i + distance) % size) for i in range(size)])


def ring_gather(value):
    middle = value.shape[0] // 2
    left = shift(value, "tensor", 1)
    right = shift(value, "tensor", -1)
    far_low = shift(left[:middle], "tensor", 1)
    far_high = shift(right[middle:], "tensor", -1)
    return [value, left, right, far_low, far_high]


def per_device(hidden, depth, qkv_weight, out_weight):
    tokens = hidden[0]
    length, width = tokens.shape
    t = lax.axis_index("tensor")
    ctx = lax.axis_index("ctx")
    depth_blocks = depth.reshape(length // TOK_BLOCK, 1, TOK_BLOCK)
    block_counts = jnp.sum((depth_blocks[:, 0] >= RECURSION).astype(jnp.int32), axis=1)
    order = jnp.arange(length // TOK_BLOCK)
    offsets = jnp.sum(
        jnp.where(order[:, None] > order[None, :], block_counts[None, :], 0), axis=1
    ).astype(jnp.int32)
    count = jnp.sum(block_counts).reshape(1)
    counts = jnp.concatenate([count] + [shift(count, "ctx", s) for s in (1, 2, 3)])
    place_ctx = jnp.concatenate([ctx.reshape(1).astype(jnp.int32), counts])
    place_both = jnp.stack([t, ctx]).astype(jnp.int32)

    rows = compact_rows(tokens, depth_blocks, offsets)
    weight = qkv_weight.reshape(qkv_weight.shape[0], -1)
    projected = []
    for half in range(2):
        own = rows[2 * half : 2 * half + 2]
        left = [shift(x, "tensor", 1) for x in own]
        right = [shift(x, "tensor", -1) for x in own]
        far = [shift(left[0], "tensor", 1), shift(right[1], "tensor", -1)]
        projected.append(project(place_both, own, left, right, far, weight))
    gathered = [lax.all_gather(p[5], "ctx", axis=0) for p in projected]
    arrived = []
    for s in range(4):
        for half in range(2):
            piece = projected[half][s]
            arrived.append(piece if s == 0 else shift(piece, "ctx", s))
    main = attend_main(place_ctx, arrived)
    last = attend_last(place_ctx, [p[4] for p in projected], gathered)
    returned = [[main[half]] for half in range(2)]
    for s in range(1, 4):
        for half in range(2):
            returned[half].append(shift(main[2 * s + half], "ctx", -s))
    groups = ring_gather(jnp.stack([last[0], last[1], main[0], main[1]]))
    for half in range(2):
        trio = jnp.stack(returned[half][1:]).reshape(6, SUB, HD)
        groups += ring_gather(trio)

    lower = out_weight[: 4 * HD]
    turned = lax.dynamic_slice_in_dim(jnp.concatenate([lower, lower]), ctx * HD, 4 * HD)
    arranged = jnp.concatenate([turned, out_weight[4 * HD :]])
    weights = []
    for distance in (0, 1, 3, 2):
        block = lax.dynamic_slice_in_dim(arranged, ((t + distance) & 3) * width, width, axis=1)
        weights.append(block if distance == 0 else shift(block, "tensor", distance))
    update = output_update(offsets, depth_blocks, groups, weights, length)
    return update[None]


def solution(mesh):
    placed = (P("dp", "ctx", "tensor"), P("dp", "ctx"), P(None, None, "tensor"), P("tensor", None))
    return jax.shard_map(
        per_device, mesh=mesh, in_specs=placed, out_specs=P("dp", "ctx", "tensor"), check_vma=False
    )
```

```python
import functools
import math

import jax
import jax.numpy as jnp
from jax import lax
from jax.experimental import pallas as pl
from jax.experimental.pallas import tpu as pltpu
from jax.sharding import PartitionSpec as P

HD = 128
RECURSION = 3
CAP = 1024
HALF = CAP // 2
SUB = CAP // 4
TOK_BLOCK = 256
WINDOW = 384
ROOM = CAP + WINDOW

score_scale = 0.25
norm_epsilon = 1e-05
head_epsilon = 1e-06
EXP2_SCALE = score_scale / math.log(2.0)
VMEM_LIMIT = 56 * 1024 * 1024

bf16 = jnp.bfloat16
f32 = jnp.float32


def cost(micros):
    return pl.CostEstimate(flops=int(micros * 1.1e9), bytes_accessed=0, transcendentals=0)


def params(**more):
    return pltpu.CompilerParams(vmem_limit_bytes=VMEM_LIMIT, **more)


def slot_onehot(depth_row, shift):
    active = depth_row >= RECURSION
    flags = jnp.broadcast_to(jnp.where(active, 1.0, 0.0), (8, TOK_BLOCK)).astype(bf16)
    before = lax.broadcasted_iota(jnp.int32, (TOK_BLOCK, TOK_BLOCK), 0)
    after = lax.broadcasted_iota(jnp.int32, (TOK_BLOCK, TOK_BLOCK), 1)
    earlier = jnp.where(before < after, 1.0, 0.0).astype(bf16)
    rank = jnp.dot(flags, earlier, preferred_element_type=f32)[0:1].astype(jnp.int32)
    slot = jnp.where(active, rank + shift, -1)
    rows = lax.broadcasted_iota(jnp.int32, (WINDOW, TOK_BLOCK), 0)
    return jnp.where(rows == slot, 1.0, 0.0).astype(bf16)


def window_start(offset):
    return pl.multiple_of((offset >> 7) << 7, 128)


def compact_kernel(offs_ref, depth_ref, tok_ref, o0, o1, buf):
    step = pl.program_id(0)

    @pl.when(step == 0)
    def _():
        buf[...] = jnp.zeros_like(buf)

    for sub in range(2):
        offset = offs_ref[step * 2 + sub]
        start = window_start(offset)
        onehot = slot_onehot(depth_ref[sub], offset - start)
        picked = jnp.dot(
            onehot,
            tok_ref[sub * TOK_BLOCK : (sub + 1) * TOK_BLOCK, :],
            preferred_element_type=f32,
        ).astype(bf16)
        buf[pl.ds(start, WINDOW), :] = buf[pl.ds(start, WINDOW), :] + picked

    @pl.when(step == pl.num_programs(0) - 1)
    def _():
        for i, o in enumerate((o0, o1)):
            o[...] = buf[i * HALF : (i + 1) * HALF, :]


def compact_rows(tokens, depth_blocks, offsets):
    length, width = tokens.shape
    steps = length // (2 * TOK_BLOCK)
    return pl.pallas_call(
        compact_kernel,
        out_shape=(jax.ShapeDtypeStruct((HALF, width), bf16),) * 2,
        grid_spec=pltpu.PrefetchScalarGridSpec(
            num_scalar_prefetch=1,
            grid=(steps,),
            in_specs=[
                pl.BlockSpec((2, 1, TOK_BLOCK), lambda i, o: (i, 0, 0)),
                pl.BlockSpec((2 * TOK_BLOCK, width), lambda i, o: (i, 0)),
            ],
            out_specs=(pl.BlockSpec((HALF, width), lambda i, o: (0, 0)),) * 2,
            scratch_shapes=[pltpu.VMEM((ROOM, width), bf16)],
        ),
        compiler_params=params(),
        cost_estimate=cost(8),
        name="compact",
    )(offsets, depth_blocks, tokens)


def project_kernel(place, x, a, b, c, d, w_ref, o0, o1, o2, o3, q4, xs, acc):
    part = pl.program_id(0)
    t = place[0]
    ctx = place[1]
    width = x.shape[1]

    @pl.when(part == 0)
    def _():
        for sub, far in enumerate((c, d)):
            low = sub * SUB
            pieces = [p[low : low + SUB, :] for p in (x, a, b)] + [far[...]]
            squares = jnp.zeros((SUB, 1), f32)
            for piece in pieces:
                wide = piece.astype(f32)
                squares = squares + jnp.sum(wide * wide, axis=1, keepdims=True)
            factor = lax.rsqrt(squares * (1.0 / (4 * width)) + norm_epsilon)
            for distance, piece in zip((0, 3, 1, 2), pieces):
                lane = pl.multiple_of(((t + distance) & 3) * width, 128)
                normed = (piece.astype(f32) * factor).astype(bf16)
                xs[low : low + SUB, pl.ds(lane, width)] = normed

    acc[...] = jnp.dot(xs[...], w_ref[0], preferred_element_type=f32)

    def column(y):
        scale = lax.rsqrt(jnp.mean(y * y, axis=1, keepdims=True) + head_epsilon)
        return (y * jnp.where(part == 2, 1.0, scale)).astype(bf16)

    outs = (o0, o1, o2, o3)
    for slot, out in enumerate(outs):
        lane = pl.multiple_of(((ctx + slot) & 3) * HD, HD)
        out[part] = column(acc[:, pl.ds(lane, HD)])
    z = column(acc[:, 4 * HD : 5 * HD])

    @pl.when(part == 0)
    def _():
        q4[...] = z

    @pl.when(part > 0)
    def _():
        for out in outs:
            out[part + 2] = z


def project(place, own, left, right, far_low, far_high, weight):
    width = own.shape[1]
    model = 4 * width
    half = pl.BlockSpec((HALF, width), lambda j, p: (0, 0))
    quarter = pl.BlockSpec((SUB, width), lambda j, p: (0, 0))
    return pl.pallas_call(
        project_kernel,
        out_shape=(jax.ShapeDtypeStruct((5, HALF, HD), bf16),) * 4
        + (jax.ShapeDtypeStruct((HALF, HD), bf16),),
        grid_spec=pltpu.PrefetchScalarGridSpec(
            num_scalar_prefetch=1,
            grid=(3,),
            in_specs=[half] * 3
            + [quarter] * 2
            + [pl.BlockSpec((1, model, 5 * HD), lambda j, p: (j, 0, 0))],
            out_specs=(pl.BlockSpec((5, HALF, HD), lambda j, p: (0, 0, 0)),) * 4
            + (pl.BlockSpec((HALF, HD), lambda j, p: (0, 0)),),
            scratch_shapes=[
                pltpu.VMEM((HALF, model), bf16),
                pltpu.VMEM((HALF, 5 * HD), f32),
            ],
        ),
        compiler_params=params(),
        cost_estimate=cost(9),
        name="project",
    )(place, own, left, right, far_low, far_high, weight)


def attend_chunk(chunk, query, count_of, ks, vs, acc):
    def add_tile(key_chunk, masked):
        scores = lax.dot_general(
            query, ks[key_chunk], (((1,), (1,)), ((), ())), preferred_element_type=f32
        )
        weights = jnp.exp2(scores * EXP2_SCALE)
        if masked:
            row = lax.broadcasted_iota(jnp.int32, (HALF, HALF), 0)
            col = lax.broadcasted_iota(jnp.int32, (HALF, HALF), 1)
            weights = jnp.where(col <= row, weights, 0.0)
        acc[...] += jnp.dot(weights.astype(bf16), vs[key_chunk], preferred_element_type=f32)

    acc[...] = jnp.zeros_like(acc)

    def body(key_chunk, carry):
        @pl.when(count_of(key_chunk >> 1) > (key_chunk & 1) * HALF)
        def _():
            add_tile(key_chunk, False)

        return carry

    lax.fori_loop(0, chunk, body, 0)
    add_tile(chunk, True)
    total = acc[:, HD:]
    return (acc[:, :HD] / jnp.where(total == 0.0, 1.0, total)).astype(bf16)


def value_rows(value, half, count):
    rows = lax.broadcasted_iota(jnp.int32, (HALF, HD), 0) + half * HALF
    return value, jnp.where(rows < count, 1.0, 0.0).astype(bf16)


def attend_main_kernel(slots, place, *refs):
    inputs, outs, (qs, ks, vs, acc) = refs[:8], refs[8:10], refs[10:]
    ctx = place[0]

    def count_of(block):
        return place[1 + ((ctx - block) & 3)]

    for s in range(4):
        for half in range(2):
            chunk = ((ctx - s) & 3) * 2 + half
            source = inputs[2 * s + half]
            qs[chunk] = source[0]
            ks[chunk] = source[1]
            value, flag = value_rows(source[2], half, place[1 + s])
            vs[chunk, :, :HD] = value
            vs[chunk, :, HD:] = flag

    for s, out in zip(slots, outs):
        count = place[1 + s]

        def body(half, carry):
            chunk = ((ctx - s) & 3) * 2 + half
            filled = count > half * HALF

            @pl.when(filled)
            def _():
                out[half] = attend_chunk(chunk, qs[chunk], count_of, ks, vs, acc)

            @pl.when(jnp.logical_not(filled))
            def _():
                out[half] = jnp.zeros((HALF, HD), bf16)

            return carry

        lax.fori_loop(0, 2, body, 0)


def vmem_specs(count):
    return [pl.BlockSpec(memory_space=pltpu.VMEM)] * count


def attend_main(slots, place, inputs):
    return pl.pallas_call(
        functools.partial(attend_main_kernel, slots),
        out_shape=(jax.ShapeDtypeStruct((2, HALF, HD), bf16),) * 2,
        in_specs=[pl.BlockSpec(memory_space=pltpu.SMEM)] + vmem_specs(8),
        out_specs=tuple(vmem_specs(2)),
        scratch_shapes=[
            pltpu.VMEM((8, HALF, HD), bf16),
            pltpu.VMEM((8, HALF, HD), bf16),
            pltpu.VMEM((8, HALF, 2 * HD), bf16),
            pltpu.VMEM((HALF, 2 * HD), f32),
        ],
        compiler_params=params(),
        cost_estimate=cost(10),
        name="attend_main",
    )(place, *inputs)


def attend_last_kernel(place, q0, q1, *refs):
    inputs, (out, ks, vs, acc) = refs[:8], refs[8:]
    ctx = place[0]

    def count_of(block):
        return place[1 + ((ctx - block) & 3)]

    for s in range(4):

        @pl.when(s <= ctx)
        def _():
            for half in range(2):
                chunk = (ctx - s) * 2 + half
                source = inputs[2 * s + half]
                ks[chunk] = source[3]
                value, flag = value_rows(source[4], half, place[1 + s])
                vs[chunk, :, :HD] = value
                vs[chunk, :, HD:] = flag

    for half, query in enumerate((q0, q1)):
        filled = place[1] > half * HALF

        @pl.when(filled)
        def _():
            out[half] = attend_chunk(ctx * 2 + half, query[...], count_of, ks, vs, acc)

        @pl.when(jnp.logical_not(filled))
        def _():
            out[half] = jnp.zeros((HALF, HD), bf16)


def attend_last(place, queries, inputs):
    return pl.pallas_call(
        attend_last_kernel,
        out_shape=jax.ShapeDtypeStruct((2, HALF, HD), bf16),
        in_specs=[pl.BlockSpec(memory_space=pltpu.SMEM)] + vmem_specs(10),
        out_specs=vmem_specs(1)[0],
        scratch_shapes=[
            pltpu.VMEM((8, HALF, HD), bf16),
            pltpu.VMEM((8, HALF, 2 * HD), bf16),
            pltpu.VMEM((HALF, 2 * HD), f32),
        ],
        compiler_params=params(),
        cost_estimate=cost(4),
        name="attend_last",
    )(place, *queries, *inputs)


def output_kernel(offs_ref, depth_ref, *refs):
    lasts, firsts, thirds, weights = refs[:4], refs[4:9], refs[9:14], refs[14:18]
    out, cbuf, rows = refs[18:]
    step = pl.program_id(0)

    @pl.when(step == 0)
    def _():
        rows[CAP:, :] = jnp.zeros((WINDOW, rows.shape[1]), bf16)
        for half in range(2):
            total = None
            for source in range(4):
                near = source < 3
                for head in range(3):
                    i = 2 * head + half
                    piece = firsts[source][i] if near else firsts[3 + i // 3][i % 3]
                    cbuf[:, head * HD : (head + 1) * HD] = piece
                cbuf[:, 3 * HD : 4 * HD] = thirds[source][half] if near else thirds[3 + half][0]
                cbuf[:, 4 * HD : 5 * HD] = lasts[source][half]
                term = jnp.dot(cbuf[...], weights[source][...], preferred_element_type=f32)
                term = term.astype(bf16).astype(f32)
                total = term if total is None else total + term
            rows[half * HALF : (half + 1) * HALF, :] = total.astype(bf16)

    for sub in range(2):
        offset = offs_ref[step * 2 + sub]
        start = window_start(offset)
        onehot = slot_onehot(depth_ref[sub], offset - start)
        spread = lax.dot_general(
            onehot,
            rows[pl.ds(start, WINDOW), :],
            (((0,), (0,)), ((), ())),
            preferred_element_type=f32,
        )
        out[sub * TOK_BLOCK : (sub + 1) * TOK_BLOCK, :] = spread.astype(bf16)


def output_update(offsets, depth_blocks, groups, weights, length):
    width = weights[0].shape[1]
    steps = length // (2 * TOK_BLOCK)

    def whole(array):
        rank = array.ndim
        return pl.BlockSpec(array.shape, lambda i, o: (0,) * rank)

    return pl.pallas_call(
        output_kernel,
        out_shape=jax.ShapeDtypeStruct((length, width), bf16),
        grid_spec=pltpu.PrefetchScalarGridSpec(
            num_scalar_prefetch=1,
            grid=(steps,),
            in_specs=[pl.BlockSpec((2, 1, TOK_BLOCK), lambda i, o: (i, 0, 0))]
            + [whole(a) for a in groups]
            + [whole(a) for a in weights],
            out_specs=pl.BlockSpec((2 * TOK_BLOCK, width), lambda i, o: (i, 0)),
            scratch_shapes=[
                pltpu.VMEM((HALF, 5 * HD), bf16),
                pltpu.VMEM((ROOM, width), bf16),
            ],
        ),
        compiler_params=params(),
        cost_estimate=cost(14),
        name="output",
    )(offsets, depth_blocks, *groups, *weights)


def shift(value, axis, distance):
    size = lax.axis_size(axis)
    return lax.ppermute(value, axis, [(i, (i + distance) % size) for i in range(size)])


def after(value, *others):
    return lax.optimization_barrier((value, others))[0]


def ring_near(value):
    return [shift(value, "tensor", 1), shift(value, "tensor", -1)]


def ring_far(near):
    middle = near[0].shape[0] // 2
    return [shift(near[0][:middle], "tensor", 1), shift(near[1][middle:], "tensor", -1)]


def per_device(hidden, depth, qkv_weight, out_weight):
    tokens = hidden[0]
    length, width = tokens.shape
    t = lax.axis_index("tensor")
    ctx = lax.axis_index("ctx")
    depth_blocks = depth.reshape(length // TOK_BLOCK, 1, TOK_BLOCK)
    block_counts = jnp.sum((depth_blocks[:, 0] >= RECURSION).astype(jnp.int32), axis=1)
    order = jnp.arange(length // TOK_BLOCK)
    offsets = jnp.sum(
        jnp.where(order[:, None] > order[None, :], block_counts[None, :], 0), axis=1
    ).astype(jnp.int32)
    count = jnp.sum(block_counts).reshape(1)
    counts = jnp.concatenate([count] + [shift(count, "ctx", s) for s in (1, 2, 3)])
    place_ctx = jnp.concatenate([ctx.reshape(1).astype(jnp.int32), counts])
    place_both = jnp.stack([t, ctx]).astype(jnp.int32)
    weight = jnp.transpose(qkv_weight, (1, 0, 2))

    rows = compact_rows(tokens, depth_blocks, offsets)
    (x0, x1), place_ctx = lax.optimization_barrier((rows, place_ctx))

    near0 = ring_near(x0)
    x1 = after(x1, near0)
    far0 = ring_far(near0)
    near1 = ring_near(x1)
    first = project(place_both, x0, *near0, *far0, weight)
    sent0 = [first[0]] + [shift(first[s], "ctx", s) for s in (1, 2, 3)]
    far1 = ring_far(near1)
    second = project(place_both, x1, *near1, *far1, weight)
    second = after(second, sent0)
    sent1 = [second[0]] + [shift(second[s], "ctx", s) for s in (1, 2, 3)]
    arrived = [piece for s in range(4) for piece in (sent0[s], sent1[s])]

    lower = out_weight[: 4 * HD]
    turned = lax.dynamic_slice_in_dim(jnp.concatenate([lower, lower]), ctx * HD, 4 * HD)
    arranged = jnp.concatenate([turned, out_weight[4 * HD :]])
    blocks = [
        lax.dynamic_slice_in_dim(arranged, ((t + distance) & 3) * width, width, axis=1)
        for distance in (0, 1, 3, 2)
    ]
    blocks = after(blocks, far1)
    weights = [blocks[0], shift(blocks[1], "tensor", 1), shift(blocks[2], "tensor", 3)]
    weights.append(shift(after(blocks[3], weights[1:]), "tensor", 2))

    arrived, weights = lax.optimization_barrier((arrived, weights))
    last = attend_last(place_ctx, (first[4], second[4]), arrived)
    lasts = [last] + ring_near(last) + [shift(last, "tensor", 2)]
    to_near, to_far = attend_main((1, 2), place_ctx, after(arrived, last))
    back = [shift(to_near, "ctx", -1), shift(to_far, "ctx", -2)]
    to_right, own = attend_main((3, 0), place_ctx, after(arrived, to_near, to_far, lasts))
    back.append(shift(to_right, "ctx", -3))
    firsts = jnp.concatenate([own, back[0], back[1]])
    near = ring_near(firsts)
    third = after(back[2], near)
    firsts = [firsts] + near + ring_far(near)
    near = ring_near(third)
    thirds = [third] + near + ring_far(near)
    update = output_update(offsets, depth_blocks, lasts + firsts + thirds, weights, length)
    return update[None]


def solution(mesh):
    placed = (P("dp", "ctx", "tensor"), P("dp", "ctx"), P(None, None, "tensor"), P("tensor", None))
    return jax.shard_map(
        per_device, mesh=mesh, in_specs=placed, out_specs=P("dp", "ctx", "tensor"), check_vma=False
    )
```

```python
import functools
import math

import jax
import jax.numpy as jnp
from jax import lax
from jax.experimental import pallas as pl
from jax.experimental.pallas import tpu as pltpu
from jax.sharding import PartitionSpec as P

HD = 128
RECURSION = 3
CAP = 1024
HALF = CAP // 2
SUB = CAP // 4
TOK_BLOCK = 256
WINDOW = TOK_BLOCK + 16
SMALL = 128
STEP_BLOCKS = 4
SHARES = 4
ROOM = CAP + WINDOW

score_scale = 0.25
norm_epsilon = 1e-05
head_epsilon = 1e-06
EXP2_SCALE = score_scale / math.log(2.0)
MEBI = 1024 * 1024

bf16 = jnp.bfloat16
f32 = jnp.float32


def cost(micros):
    return pl.CostEstimate(flops=int(micros * 1.1e9), bytes_accessed=0, transcendentals=0)


def params(mebibytes):
    return pltpu.CompilerParams(vmem_limit_bytes=mebibytes * MEBI)


def fill_slots(depth_ref, slots):
    active = depth_ref[...] >= RECURSION
    flags = jnp.where(active, 1.0, 0.0).astype(bf16)
    before = lax.broadcasted_iota(jnp.int32, (TOK_BLOCK, TOK_BLOCK), 0)
    after_it = lax.broadcasted_iota(jnp.int32, (TOK_BLOCK, TOK_BLOCK), 1)
    earlier = jnp.where(before < after_it, 1.0, 0.0).astype(bf16)
    rank = jnp.dot(flags, earlier, preferred_element_type=f32).astype(jnp.int32)
    slots[...] = jnp.where(active, rank, -2 * CAP)


def window_onehot(slots, block, shift_by, window):
    rows = lax.broadcasted_iota(jnp.int32, (window, TOK_BLOCK), 0)
    return jnp.where(rows == slots[pl.ds(block, 1), :] + shift_by, 1.0, 0.0).astype(bf16)


def by_window(offs_ref, block, run):
    low, high = offs_ref[block], offs_ref[block + 1]
    start = pl.multiple_of((low >> 4) << 4, 16)

    @pl.when(high - start <= SMALL)
    def _():
        run(start, low - start, SMALL)

    @pl.when(high - start > SMALL)
    def _():
        run(start, low - start, WINDOW)


def compact_kernel(offs_ref, depth_ref, tok_ref, o0, o1, buf, slots):
    step = pl.program_id(0)

    @pl.when(step == 0)
    def _():
        buf[...] = jnp.zeros_like(buf)
        fill_slots(depth_ref, slots)

    def body(sub, carry):
        block = step * STEP_BLOCKS + sub
        at = pl.multiple_of(sub * TOK_BLOCK, TOK_BLOCK)

        def run(start, shift_by, window):
            picked = jnp.dot(
                window_onehot(slots, block, shift_by, window),
                tok_ref[pl.ds(at, TOK_BLOCK), :],
                preferred_element_type=f32,
            ).astype(bf16)
            buf[pl.ds(start, window), :] = buf[pl.ds(start, window), :] + picked

        by_window(offs_ref, block, run)
        return carry

    lax.fori_loop(0, STEP_BLOCKS, body, 0)

    @pl.when(step == pl.num_programs(0) - 1)
    def _():
        for i, o in enumerate((o0, o1)):
            o[...] = buf[i * HALF : (i + 1) * HALF, :]


def compact_rows(tokens, depth_blocks, offsets):
    length, width = tokens.shape
    blocks = length // TOK_BLOCK
    rows = STEP_BLOCKS * TOK_BLOCK
    return pl.pallas_call(
        compact_kernel,
        out_shape=(jax.ShapeDtypeStruct((HALF, width), bf16),) * 2,
        grid_spec=pltpu.PrefetchScalarGridSpec(
            num_scalar_prefetch=1,
            grid=(length // rows,),
            in_specs=[
                pl.BlockSpec((blocks, TOK_BLOCK), lambda i, o: (0, 0)),
                pl.BlockSpec((rows, width), lambda i, o: (i, 0)),
            ],
            out_specs=(pl.BlockSpec((HALF, width), lambda i, o: (0, 0)),) * 2,
            scratch_shapes=[
                pltpu.VMEM((ROOM, width), bf16),
                pltpu.VMEM((blocks, TOK_BLOCK), jnp.int32),
            ],
        ),
        compiler_params=params(12),
        cost_estimate=cost(8),
        name="compact",
    )(offsets, depth_blocks, tokens)


def project_kernel(place, x, a, b, c, d, w_ref, o0, o1, o2, o3, q4, xs, acc):
    t = place[0]
    ctx = place[1]
    width = x.shape[1]
    for sub, far in enumerate((c, d)):
        low = sub * SUB
        pieces = [p[low : low + SUB, :] for p in (x, a, b)] + [far[...]]
        squares = jnp.zeros((SUB, 1), f32)
        for piece in pieces:
            wide = piece.astype(f32)
            squares = squares + jnp.sum(wide * wide, axis=1, keepdims=True)
        factor = lax.rsqrt(squares * (1.0 / (4 * width)) + norm_epsilon)
        for distance, piece in zip((0, 3, 1, 2), pieces):
            lane = pl.multiple_of(((t + distance) & 3) * width, 128)
            normed = (piece.astype(f32) * factor).astype(bf16)
            xs[low : low + SUB, pl.ds(lane, width)] = normed

    outs = (o0, o1, o2, o3)

    def body(part, carry):
        acc[...] = jnp.dot(xs[...], w_ref[part], preferred_element_type=f32)

        def column(y):
            scale = lax.rsqrt(jnp.mean(y * y, axis=1, keepdims=True) + head_epsilon)
            return (y * jnp.where(part == 2, 1.0, scale)).astype(bf16)

        for slot, out in enumerate(outs):
            lane = pl.multiple_of(((ctx + slot) & 3) * HD, HD)
            out[part] = column(acc[:, pl.ds(lane, HD)])
        z = column(acc[:, 4 * HD : 5 * HD])

        @pl.when(part == 0)
        def _():
            q4[...] = z

        @pl.when(part > 0)
        def _():
            for out in outs:
                out[part + 2] = z

        return carry

    lax.fori_loop(0, 3, body, 0)


def project(place, own, left, right, far_low, far_high, weight, micros):
    width = own.shape[1]
    return pl.pallas_call(
        project_kernel,
        out_shape=(jax.ShapeDtypeStruct((5, HALF, HD), bf16),) * 4
        + (jax.ShapeDtypeStruct((HALF, HD), bf16),),
        in_specs=[pl.BlockSpec(memory_space=pltpu.SMEM)] + vmem_specs(6),
        out_specs=tuple(vmem_specs(5)),
        scratch_shapes=[
            pltpu.VMEM((HALF, 4 * width), bf16),
            pltpu.VMEM((HALF, 5 * HD), f32),
        ],
        compiler_params=params(16),
        cost_estimate=cost(micros),
        name="project",
    )(place, own, left, right, far_low, far_high, weight)


def attend_block(block, count, query, count_of, ks, vs, acc):
    def add_tiles(chunk, base=None):
        scores = [
            jnp.dot(query[at : at + HALF, :], ks[chunk], preferred_element_type=f32)
            for at in (0, HALF)
        ]
        for at, score in zip((0, HALF), scores):
            weights = jnp.exp2(score * EXP2_SCALE)
            if base is not None:
                row = lax.broadcasted_iota(jnp.int32, (HALF, HALF), 0) + (at - base)
                col = lax.broadcasted_iota(jnp.int32, (HALF, HALF), 1)
                weights = jnp.where(col <= row, weights, 0.0)
            acc[at : at + HALF, :] += jnp.dot(
                weights.astype(bf16), vs[chunk], preferred_element_type=f32
            )

    acc[...] = jnp.zeros_like(acc)

    @pl.when(count > 0)
    def _():
        def earlier(chunk, carry):
            @pl.when(count_of(chunk >> 1) > (chunk & 1) * HALF)
            def _():
                add_tiles(chunk)

            return carry

        def same(half, carry):
            @pl.when(count > half * HALF)
            def _():
                add_tiles(2 * block + half, half * HALF)

            return carry

        lax.fori_loop(0, 2 * block, earlier, 0)
        lax.fori_loop(0, 2, same, 0)


def context_of(acc, low):
    total = acc[low : low + HALF, HD:]
    return (acc[low : low + HALF, :HD] / jnp.where(total == 0.0, 1.0, total)).astype(bf16)


def place_keys(chunk, half, count, key, value, ks, vs):
    @pl.when(count > half * HALF)
    def _():
        ks[chunk] = key.T
        rows = lax.broadcasted_iota(jnp.int32, (HALF, HD), 0) + half * HALF
        vs[chunk, :, :HD] = value
        vs[chunk, :, HD:] = jnp.where(rows < count, 1.0, 0.0).astype(bf16)


def attend_main_kernel(first_slot, place, *refs):
    inputs, outs, (qs, ks, vs, cs, acc) = refs[:8], refs[8:10], refs[10:]
    ctx = place[0]

    def count_of(block):
        return place[1 + ((ctx - block) & 3)]

    for s in range(4):
        block = (ctx - s) & 3
        for half in range(2):
            source = inputs[2 * s + half]
            qs[s, half * HALF : (half + 1) * HALF] = source[0]
            place_keys(2 * block + half, half, place[1 + s], source[1], source[2], ks, vs)

    def body(i, carry):
        s = (first_slot + i) & 3
        attend_block((ctx - s) & 3, place[1 + s], qs.at[s], count_of, ks, vs, acc)
        for half in range(2):
            cs[i, half] = context_of(acc, half * HALF)
        return carry

    lax.fori_loop(0, 2, body, 0)
    for i, out in enumerate(outs):
        out[...] = cs[i]


def vmem_specs(count):
    return [pl.BlockSpec(memory_space=pltpu.VMEM)] * count


def attend_main(first_slot, place, inputs):
    return pl.pallas_call(
        functools.partial(attend_main_kernel, first_slot),
        out_shape=(jax.ShapeDtypeStruct((2, HALF, HD), bf16),) * 2,
        in_specs=[pl.BlockSpec(memory_space=pltpu.SMEM)] + vmem_specs(8),
        out_specs=tuple(vmem_specs(2)),
        scratch_shapes=[
            pltpu.VMEM((4, CAP, HD), bf16),
            pltpu.VMEM((8, HD, HALF), bf16),
            pltpu.VMEM((8, HALF, 2 * HD), bf16),
            pltpu.VMEM((2, 2, HALF, HD), bf16),
            pltpu.VMEM((CAP, 2 * HD), f32),
        ],
        compiler_params=params(16),
        cost_estimate=cost(10),
        name="attend_main",
    )(place, *inputs)


def attend_last_kernel(place, q0, q1, *refs):
    inputs, (out, qs, ks, vs, acc) = refs[:8], refs[8:]
    ctx = place[0]

    def count_of(block):
        return place[1 + ((ctx - block) & 3)]

    for s in range(4):

        @pl.when(s <= ctx)
        def _():
            for half in range(2):
                source = inputs[2 * s + half]
                chunk = (ctx - s) * 2 + half
                place_keys(chunk, half, place[1 + s], source[3], source[4], ks, vs)

    qs[:HALF, :] = q0[...]
    qs[HALF:, :] = q1[...]
    attend_block(ctx, place[1], qs, count_of, ks, vs, acc)
    for half in range(2):
        out[half] = context_of(acc, half * HALF)


def attend_last(place, queries, inputs):
    return pl.pallas_call(
        attend_last_kernel,
        out_shape=jax.ShapeDtypeStruct((2, HALF, HD), bf16),
        in_specs=[pl.BlockSpec(memory_space=pltpu.SMEM)] + vmem_specs(10),
        out_specs=vmem_specs(1)[0],
        scratch_shapes=[
            pltpu.VMEM((CAP, HD), bf16),
            pltpu.VMEM((8, HD, HALF), bf16),
            pltpu.VMEM((8, HALF, 2 * HD), bf16),
            pltpu.VMEM((CAP, 2 * HD), f32),
        ],
        compiler_params=params(16),
        cost_estimate=cost(4),
        name="attend_last",
    )(place, *queries, *inputs)


def group_term(pieces, weight, cbuf):
    for i, piece in enumerate(pieces):
        cbuf[:, i * HD : (i + 1) * HD] = piece
    term = jnp.dot(cbuf[...], weight, preferred_element_type=f32)
    return term.astype(bf16).astype(f32)


def whole_block(gathered, which, dp):
    places = []
    for share in range(SHARES):
        other = (dp & (SHARES - 1)) ^ share
        places.append((other >> 1) + 2 * (other & 1))
    parts = [gathered[place, which, slot] for slot in range(5) for place in places]
    return jnp.concatenate(parts, axis=0)


def near_terms_kernel(place, *refs):
    lasts, firsts, thirds, (own, gathered), (out, cbuf) = (
        refs[:3],
        refs[3:6],
        refs[6:9],
        refs[9:11],
        refs[11:],
    )
    for source, (last, first, third) in enumerate(zip(lasts, firsts, thirds)):
        if source == 0:
            starts = [pl.multiple_of(((place[0] + slot) & 3) * HD, HD) for slot in range(4)]
            parts = [own[pl.ds(start, HD), :] for start in starts]
            weight = jnp.concatenate(parts + [own[4 * HD :, :]], axis=0)
        else:
            weight = whole_block(gathered, source - 1, place[5])
        for half in range(2):
            at = slice(half * HALF, (half + 1) * HALF)
            pieces = [first[2 * head + half] for head in range(3)] + [third[half], last[half]]
            term = group_term(pieces, weight, cbuf)
            out[at, :] = term if source == 0 else out[at, :] + term


def near_terms(place, lasts, firsts, thirds, own_block, gathered):
    return pl.pallas_call(
        near_terms_kernel,
        out_shape=jax.ShapeDtypeStruct((CAP, own_block.shape[1]), f32),
        in_specs=[pl.BlockSpec(memory_space=pltpu.SMEM)] + vmem_specs(11),
        out_specs=vmem_specs(1)[0],
        scratch_shapes=[pltpu.VMEM((HALF, 5 * HD), bf16)],
        compiler_params=params(12),
        cost_estimate=cost(5),
        name="near_terms",
    )(place, *lasts, *firsts, *thirds, own_block, gathered)


def output_kernel(offs_ref, depth_ref, last, f_low, f_high, t_low, t_high, gathered, near, out, *scratch):
    cbuf, rows, slots = scratch
    step = pl.program_id(0)

    @pl.when(step == 0)
    def _():
        fill_slots(depth_ref, slots)
        rows[CAP:, :] = jnp.zeros((WINDOW, rows.shape[1]), bf16)
        firsts = [f_low[i] for i in range(3)] + [f_high[i] for i in range(3)]
        thirds = [t_low[0], t_high[0]]
        weight = whole_block(gathered, 2, offs_ref[depth_ref.shape[0] + 1])
        for half in range(2):
            at = slice(half * HALF, (half + 1) * HALF)
            pieces = [firsts[2 * head + half] for head in range(3)] + [thirds[half], last[half]]
            rows[at, :] = (near[at, :] + group_term(pieces, weight, cbuf)).astype(bf16)

    def body(sub, carry):
        block = step * STEP_BLOCKS + sub
        at = pl.multiple_of(sub * TOK_BLOCK, TOK_BLOCK)

        def run(start, shift_by, window):
            spread = lax.dot_general(
                window_onehot(slots, block, shift_by, window),
                rows[pl.ds(start, window), :],
                (((0,), (0,)), ((), ())),
                preferred_element_type=f32,
            )
            out[pl.ds(at, TOK_BLOCK), :] = spread.astype(bf16)

        by_window(offs_ref, block, run)
        return carry

    lax.fori_loop(0, STEP_BLOCKS, body, 0)


def output_update(offsets, depth_blocks, pieces, gathered, near, length):
    width = near.shape[1]
    blocks = length // TOK_BLOCK
    rows = STEP_BLOCKS * TOK_BLOCK

    operands = (depth_blocks, *pieces, gathered, near)
    return pl.pallas_call(
        output_kernel,
        out_shape=jax.ShapeDtypeStruct((length, width), bf16),
        grid_spec=pltpu.PrefetchScalarGridSpec(
            num_scalar_prefetch=1,
            grid=(length // rows,),
            in_specs=vmem_specs(len(operands)),
            out_specs=pl.BlockSpec((rows, width), lambda i, o: (i, 0)),
            scratch_shapes=[
                pltpu.VMEM((HALF, 5 * HD), bf16),
                pltpu.VMEM((ROOM, width), bf16),
                pltpu.VMEM((blocks, TOK_BLOCK), jnp.int32),
            ],
        ),
        compiler_params=params(16),
        cost_estimate=cost(8),
        name="output",
    )(offsets, *operands)


def shift(value, axis, distance):
    size = lax.axis_size(axis)
    return lax.ppermute(value, axis, [(i, (i + distance) % size) for i in range(size)])


def swap(value, axis, bit):
    return lax.ppermute(value, axis, [(i, i ^ bit) for i in range(lax.axis_size(axis))])


def after(value, *others):
    return lax.optimization_barrier((value, others))[0]


def ring_near(value):
    return [shift(value, "tensor", 1), shift(value, "tensor", -1)]


def ring_far(near):
    middle = near[0].shape[0] // 2
    return [shift(near[0][:middle], "tensor", 1), shift(near[1][middle:], "tensor", -1)]


def per_device(hidden, depth, qkv_weight, out_weight):
    tokens = hidden[0]
    length, width = tokens.shape
    t = lax.axis_index("tensor")
    ctx = lax.axis_index("ctx")
    depth_blocks = depth.reshape(length // TOK_BLOCK, TOK_BLOCK)
    block_counts = jnp.sum((depth_blocks >= RECURSION).astype(jnp.int32), axis=1)
    ends = jnp.arange(length // TOK_BLOCK + 1)
    offsets = jnp.sum(
        jnp.where(ends[:, None] > ends[None, :-1], block_counts[None, :], 0), axis=1
    ).astype(jnp.int32)
    count = jnp.sum(block_counts).reshape(1)
    place_both = jnp.stack([t, ctx]).astype(jnp.int32)
    weight = jnp.transpose(qkv_weight, (1, 0, 2))

    x0, x1 = compact_rows(tokens, depth_blocks, offsets)


    def column_block(rows, distance):
        start = ((t + distance) & 3) * width
        return lax.dynamic_slice_in_dim(rows, start, width, axis=rows.ndim - 1)

    own_block = column_block(out_weight, 0)
    dp = lax.axis_index("dp")
    shares = out_weight.reshape(5, SHARES, HD // SHARES, out_weight.shape[1])
    shares = lax.dynamic_slice_in_dim(shares, dp & (SHARES - 1), 1, axis=1)[:, 0]
    turned = lax.dynamic_slice_in_dim(jnp.concatenate([shares[:4], shares[:4]]), ctx, 4)
    shares = jnp.concatenate([turned, shares[4:]])

    near0 = ring_near(x0)
    count = after(count, near0)
    others = [shift(count, "ctx", s) for s in (1, 2, 3)]
    far0 = ring_far(near0)
    x1, others = after((x1, others), far0)
    place_ctx = jnp.stack([ctx.astype(jnp.int32), count[0], *[o[0] for o in others], dp.astype(jnp.int32)])
    near1 = ring_near(x1)
    first = project(place_both, x0, *near0, *far0, weight, 9)
    sent0 = [first[0]] + [shift(first[s], "ctx", s) for s in (1, 2, 3)]
    far1 = ring_far(after(near1, first))
    second = project(place_both, x1, *near1, *far1, weight, 9)
    second, shares = after((second, shares), sent0)
    moved = [shift(column_block(shares, d), "tensor", d) for d in (1, 3, 2)]
    gathered = jnp.stack(moved)[None]
    for bit in (2, 1):
        gathered = jnp.concatenate([gathered, swap(gathered, "dp", bit)])
    sent1 = [second[0]] + [shift(second[s], "ctx", s) for s in (1, 2, 3)]
    arrived = [piece for s in range(4) for piece in (sent0[s], sent1[s])]

    last = attend_last(place_ctx, (first[4], second[4]), arrived)
    lasts = [last] + ring_near(last) + [shift(last, "tensor", 2)]
    to_near, to_far = attend_main(1, after(place_ctx, last), arrived)
    back = [shift(to_near, "ctx", -1), shift(to_far, "ctx", -2)]
    to_right, own = attend_main(3, after(place_ctx, to_near, to_far, lasts), arrived)
    back.append(shift(to_right, "ctx", -3))
    own, lasts, gathered = lax.optimization_barrier((own, lasts, gathered))
    firsts = jnp.concatenate([own, back[0], back[1]])
    near = ring_near(firsts)
    third = after(back[2], near)
    firsts = [firsts] + near + ring_far(near)
    near = ring_near(third)
    thirds = [third] + near + ring_far(near)
    summed = near_terms(place_ctx, lasts[:3], firsts[:3], thirds[:3], own_block, gathered)
    pieces = [lasts[3]] + firsts[3:] + thirds[3:]
    update = output_update(
        jnp.concatenate([offsets, dp.reshape(1).astype(jnp.int32)]),
        depth_blocks,
        pieces,
        gathered,
        summed,
        length,
    )
    return update[None]


def solution(mesh):
    placed = (P("dp", "ctx", "tensor"), P("dp", "ctx"), P(None, None, "tensor"), P("tensor", None))
    return jax.shard_map(
        per_device, mesh=mesh, in_specs=placed, out_specs=P("dp", "ctx", "tensor"), check_vma=False
    )
```

```python
import functools
import math

import jax
import jax.numpy as jnp
from jax import lax
from jax.experimental import pallas as pl
from jax.experimental.pallas import tpu as pltpu
from jax.sharding import PartitionSpec as P

HD = 128
RECURSION = 3
CAP = 1024
HALF = CAP // 2
SUB = CAP // 4
TOK_BLOCK = 256
WINDOW = TOK_BLOCK + 16
SMALL = 128
STEP_BLOCKS = 4
SHARES = 4
ROOM = CAP + WINDOW

score_scale = 0.25
norm_epsilon = 1e-05
head_epsilon = 1e-06
EXP2_SCALE = score_scale / math.log(2.0)
MEBI = 1024 * 1024

bf16 = jnp.bfloat16
f32 = jnp.float32


def cost(micros):
    return pl.CostEstimate(flops=int(micros * 1.1e9), bytes_accessed=0, transcendentals=0)


def params(mebibytes):
    return pltpu.CompilerParams(vmem_limit_bytes=mebibytes * MEBI)


def fill_slots(depth_ref, slots):
    active = depth_ref[...] >= RECURSION
    flags = jnp.where(active, 1.0, 0.0).astype(bf16)
    before = lax.broadcasted_iota(jnp.int32, (TOK_BLOCK, TOK_BLOCK), 0)
    after_it = lax.broadcasted_iota(jnp.int32, (TOK_BLOCK, TOK_BLOCK), 1)
    earlier = jnp.where(before < after_it, 1.0, 0.0).astype(bf16)
    rank = jnp.dot(flags, earlier, preferred_element_type=f32).astype(jnp.int32)
    slots[...] = jnp.where(active, rank, -2 * CAP)


def window_onehot(slots, block, shift_by, window):
    rows = lax.broadcasted_iota(jnp.int32, (window, TOK_BLOCK), 0)
    return jnp.where(rows == slots[pl.ds(block, 1), :] + shift_by, 1.0, 0.0).astype(bf16)


def by_window(offs_ref, block, run):
    low, high = offs_ref[block], offs_ref[block + 1]
    start = pl.multiple_of((low >> 4) << 4, 16)

    @pl.when(high - start <= SMALL)
    def _():
        run(start, low - start, SMALL)

    @pl.when(high - start > SMALL)
    def _():
        run(start, low - start, WINDOW)


def compact_kernel(offs_ref, depth_ref, tok_ref, o0, o1, squares, buf, slots):
    step = pl.program_id(0)

    @pl.when(step == 0)
    def _():
        buf[...] = jnp.zeros_like(buf)
        fill_slots(depth_ref, slots)

    def body(sub, carry):
        block = step * STEP_BLOCKS + sub
        at = pl.multiple_of(sub * TOK_BLOCK, TOK_BLOCK)

        def run(start, shift_by, window):
            picked = jnp.dot(
                window_onehot(slots, block, shift_by, window),
                tok_ref[pl.ds(at, TOK_BLOCK), :],
                preferred_element_type=f32,
            ).astype(bf16)
            buf[pl.ds(start, window), :] = buf[pl.ds(start, window), :] + picked

        by_window(offs_ref, block, run)
        return carry

    lax.fori_loop(0, STEP_BLOCKS, body, 0)

    @pl.when(step == pl.num_programs(0) - 1)
    def _():
        ones = jnp.ones((8, buf.shape[1]), bf16)
        for i, o in enumerate((o0, o1)):
            rows = buf[i * HALF : (i + 1) * HALF, :]
            o[...] = rows
            wide = rows.astype(f32)
            square = wide * wide
            high = square.astype(bf16)
            low = (square - high.astype(f32)).astype(bf16)
            squares[:, i * HALF : (i + 1) * HALF] = sum(
                lax.dot_general(ones, part, (((1,), (1,)), ((), ())), preferred_element_type=f32)
                for part in (high, low)
            )


def compact_rows(tokens, depth_blocks, offsets):
    length, width = tokens.shape
    blocks = length // TOK_BLOCK
    rows = STEP_BLOCKS * TOK_BLOCK
    return pl.pallas_call(
        compact_kernel,
        out_shape=(jax.ShapeDtypeStruct((HALF, width), bf16),) * 2
        + (jax.ShapeDtypeStruct((8, CAP), f32),),
        grid_spec=pltpu.PrefetchScalarGridSpec(
            num_scalar_prefetch=1,
            grid=(length // rows,),
            in_specs=[
                pl.BlockSpec((blocks, TOK_BLOCK), lambda i, o: (0, 0)),
                pl.BlockSpec((rows, width), lambda i, o: (i, 0)),
            ],
            out_specs=(pl.BlockSpec((HALF, width), lambda i, o: (0, 0)),) * 2
            + (pl.BlockSpec((8, CAP), lambda i, o: (0, 0)),),
            scratch_shapes=[
                pltpu.VMEM((ROOM, width), bf16),
                pltpu.VMEM((blocks, TOK_BLOCK), jnp.int32),
            ],
        ),
        compiler_params=params(12),
        cost_estimate=cost(8),
        name="compact",
    )(offsets, depth_blocks, tokens)


def normed_rows(piece, squares, low, model):
    total = squares[:, low : low + piece.shape[0]].T[:, 0:1]
    factor = lax.rsqrt(total * (1.0 / model) + norm_epsilon)
    return (piece[...].astype(f32) * factor).astype(bf16)


def source_rows(t, distance, width):
    return pl.ds(pl.multiple_of(((t + distance) & 3) * width, 128), width)


def project_near_kernel(place, squares, x, a, b, w_ref, out, x0, x1, x2):
    t = place[0]
    width = x.shape[1]
    for piece, held in zip((x, a, b), (x0, x1, x2)):
        held[...] = normed_rows(piece, squares, 0, 4 * width)

    def body(part, carry):
        total = None
        for distance, held in zip((0, 3, 1), (x0, x1, x2)):
            term = jnp.dot(
                held[...],
                w_ref[part, source_rows(t, distance, width), :],
                preferred_element_type=f32,
            )
            total = term if total is None else total + term
        out[part] = total
        return carry

    lax.fori_loop(0, 3, body, 0)


def project_near(place, squares, own, left, right, weight):
    width = own.shape[1]
    return pl.pallas_call(
        project_near_kernel,
        out_shape=jax.ShapeDtypeStruct((3, HALF, 5 * HD), f32),
        in_specs=[pl.BlockSpec(memory_space=pltpu.SMEM)] + vmem_specs(5),
        out_specs=vmem_specs(1)[0],
        scratch_shapes=[pltpu.VMEM((HALF, width), bf16)] * 3,
        compiler_params=params(12),
        cost_estimate=cost(8),
        name="project_near",
    )(place, squares, own, left, right, weight)


def project_kernel(place, squares, near, c, d, w_ref, o0, o1, o2, o3, q4, xs, acc):
    t = place[0]
    ctx = place[1]
    width = c.shape[1]
    for sub, far in enumerate((c, d)):
        xs[sub * SUB : (sub + 1) * SUB, :] = normed_rows(far, squares, sub * SUB, 4 * width)

    outs = (o0, o1, o2, o3)

    def body(part, carry):
        acc[...] = near[part] + jnp.dot(
            xs[...], w_ref[part, source_rows(t, 2, width), :], preferred_element_type=f32
        )

        def column(y):
            scale = lax.rsqrt(jnp.mean(y * y, axis=1, keepdims=True) + head_epsilon)
            return (y * jnp.where(part == 2, 1.0, scale)).astype(bf16)

        for slot, out in enumerate(outs):
            lane = pl.multiple_of(((ctx + slot) & 3) * HD, HD)
            out[part] = column(acc[:, pl.ds(lane, HD)])
        z = column(acc[:, 4 * HD : 5 * HD])

        @pl.when(part == 0)
        def _():
            q4[...] = z

        @pl.when(part > 0)
        def _():
            for out in outs:
                out[part + 2] = z

        return carry

    lax.fori_loop(0, 3, body, 0)


def project(place, squares, near, far_low, far_high, weight):
    width = far_low.shape[1]
    return pl.pallas_call(
        project_kernel,
        out_shape=(jax.ShapeDtypeStruct((5, HALF, HD), bf16),) * 4
        + (jax.ShapeDtypeStruct((HALF, HD), bf16),),
        in_specs=[pl.BlockSpec(memory_space=pltpu.SMEM)] + vmem_specs(5),
        out_specs=tuple(vmem_specs(5)),
        scratch_shapes=[
            pltpu.VMEM((HALF, width), bf16),
            pltpu.VMEM((HALF, 5 * HD), f32),
        ],
        compiler_params=params(12),
        cost_estimate=cost(5),
        name="project",
    )(place, squares, near, far_low, far_high, weight)


def attend_block(block, count, query, count_of, ks, vs, acc):
    def add_tiles(chunk, base=None):
        scores = [
            jnp.dot(query[at : at + HALF, :], ks[chunk], preferred_element_type=f32)
            for at in (0, HALF)
        ]
        for at, score in zip((0, HALF), scores):
            weights = jnp.exp2(score * EXP2_SCALE)
            if base is not None:
                row = lax.broadcasted_iota(jnp.int32, (HALF, HALF), 0) + (at - base)
                col = lax.broadcasted_iota(jnp.int32, (HALF, HALF), 1)
                weights = jnp.where(col <= row, weights, 0.0)
            acc[at : at + HALF, :] += jnp.dot(
                weights.astype(bf16), vs[chunk], preferred_element_type=f32
            )

    acc[...] = jnp.zeros_like(acc)

    @pl.when(count > 0)
    def _():
        def earlier(chunk, carry):
            @pl.when(count_of(chunk >> 1) > (chunk & 1) * HALF)
            def _():
                add_tiles(chunk)

            return carry

        def same(half, carry):
            @pl.when(count > half * HALF)
            def _():
                add_tiles(2 * block + half, half * HALF)

            return carry

        lax.fori_loop(0, 2 * block, earlier, 0)
        lax.fori_loop(0, 2, same, 0)


def context_of(acc, low):
    total = acc[low : low + HALF, HD:]
    return (acc[low : low + HALF, :HD] / jnp.where(total == 0.0, 1.0, total)).astype(bf16)


def place_keys(chunk, half, count, key, value, ks, vs):
    @pl.when(count > half * HALF)
    def _():
        ks[chunk] = key.T
        rows = lax.broadcasted_iota(jnp.int32, (HALF, HD), 0) + half * HALF
        vs[chunk, :, :HD] = value
        vs[chunk, :, HD:] = jnp.where(rows < count, 1.0, 0.0).astype(bf16)


def attend_main_kernel(first_slot, place, *refs):
    inputs, outs, (qs, ks, vs, cs, acc) = refs[:8], refs[8:10], refs[10:]
    ctx = place[0]

    def count_of(block):
        return place[1 + ((ctx - block) & 3)]

    for s in range(4):
        block = (ctx - s) & 3
        for half in range(2):
            source = inputs[2 * s + half]
            qs[s, half * HALF : (half + 1) * HALF] = source[0]
            place_keys(2 * block + half, half, place[1 + s], source[1], source[2], ks, vs)

    def body(i, carry):
        s = (first_slot + i) & 3
        attend_block((ctx - s) & 3, place[1 + s], qs.at[s], count_of, ks, vs, acc)
        for half in range(2):
            cs[i, half] = context_of(acc, half * HALF)
        return carry

    lax.fori_loop(0, 2, body, 0)
    for i, out in enumerate(outs):
        out[...] = cs[i]


def vmem_specs(count):
    return [pl.BlockSpec(memory_space=pltpu.VMEM)] * count


def attend_main(first_slot, place, inputs):
    return pl.pallas_call(
        functools.partial(attend_main_kernel, first_slot),
        out_shape=(jax.ShapeDtypeStruct((2, HALF, HD), bf16),) * 2,
        in_specs=[pl.BlockSpec(memory_space=pltpu.SMEM)] + vmem_specs(8),
        out_specs=tuple(vmem_specs(2)),
        scratch_shapes=[
            pltpu.VMEM((4, CAP, HD), bf16),
            pltpu.VMEM((8, HD, HALF), bf16),
            pltpu.VMEM((8, HALF, 2 * HD), bf16),
            pltpu.VMEM((2, 2, HALF, HD), bf16),
            pltpu.VMEM((CAP, 2 * HD), f32),
        ],
        compiler_params=params(16),
        cost_estimate=cost(10),
        name="attend_main",
    )(place, *inputs)


def attend_last_kernel(place, q0, q1, *refs):
    inputs, (out, qs, ks, vs, acc) = refs[:8], refs[8:]
    ctx = place[0]

    def count_of(block):
        return place[1 + ((ctx - block) & 3)]

    for s in range(4):

        @pl.when(s <= ctx)
        def _():
            for half in range(2):
                source = inputs[2 * s + half]
                chunk = (ctx - s) * 2 + half
                place_keys(chunk, half, place[1 + s], source[3], source[4], ks, vs)

    qs[:HALF, :] = q0[...]
    qs[HALF:, :] = q1[...]
    attend_block(ctx, place[1], qs, count_of, ks, vs, acc)
    for half in range(2):
        out[half] = context_of(acc, half * HALF)


def attend_last(place, queries, inputs):
    return pl.pallas_call(
        attend_last_kernel,
        out_shape=jax.ShapeDtypeStruct((2, HALF, HD), bf16),
        in_specs=[pl.BlockSpec(memory_space=pltpu.SMEM)] + vmem_specs(10),
        out_specs=vmem_specs(1)[0],
        scratch_shapes=[
            pltpu.VMEM((CAP, HD), bf16),
            pltpu.VMEM((8, HD, HALF), bf16),
            pltpu.VMEM((8, HALF, 2 * HD), bf16),
            pltpu.VMEM((CAP, 2 * HD), f32),
        ],
        compiler_params=params(16),
        cost_estimate=cost(4),
        name="attend_last",
    )(place, *queries, *inputs)


def group_term(pieces, weight, cbuf):
    for i, piece in enumerate(pieces):
        cbuf[:, i * HD : (i + 1) * HD] = piece
    term = jnp.dot(cbuf[...], weight, preferred_element_type=f32)
    return term.astype(bf16).astype(f32)


def whole_block(gathered, which, dp):
    places = []
    for share in range(SHARES):
        other = (dp & (SHARES - 1)) ^ share
        places.append((other >> 1, (other & 1) == 1))
    here, there = gathered
    parts = [
        jnp.where(swapped, there[place, which, slot], here[place, which, slot])
        for slot in range(5)
        for place, swapped in places
    ]
    return jnp.concatenate(parts, axis=0)


def near_terms_kernel(place, *refs):
    lasts, firsts, thirds, (own, *gathered), (out, cbuf) = (
        refs[:3],
        refs[3:6],
        refs[6:9],
        refs[9:12],
        refs[12:],
    )
    for source, (last, first, third) in enumerate(zip(lasts, firsts, thirds)):
        if source == 0:
            starts = [pl.multiple_of(((place[0] + slot) & 3) * HD, HD) for slot in range(4)]
            parts = [own[pl.ds(start, HD), :] for start in starts]
            weight = jnp.concatenate(parts + [own[4 * HD :, :]], axis=0)
        else:
            weight = whole_block(gathered, source - 1, place[5])
        for half in range(2):
            at = slice(half * HALF, (half + 1) * HALF)
            pieces = [first[2 * head + half] for head in range(3)] + [third[half], last[half]]
            term = group_term(pieces, weight, cbuf)
            out[at, :] = term if source == 0 else out[at, :] + term


def near_terms(place, lasts, firsts, thirds, own_block, gathered):
    return pl.pallas_call(
        near_terms_kernel,
        out_shape=jax.ShapeDtypeStruct((CAP, own_block.shape[1]), f32),
        in_specs=[pl.BlockSpec(memory_space=pltpu.SMEM)] + vmem_specs(12),
        out_specs=vmem_specs(1)[0],
        scratch_shapes=[pltpu.VMEM((HALF, 5 * HD), bf16)],
        compiler_params=params(12),
        cost_estimate=cost(5),
        name="near_terms",
    )(place, *lasts, *firsts, *thirds, own_block, *gathered)


def output_kernel(offs_ref, depth_ref, last, f_low, f_high, t_low, t_high, here, there, near, out, *scratch):
    cbuf, rows, slots = scratch
    step = pl.program_id(0)

    @pl.when(step == 0)
    def _():
        fill_slots(depth_ref, slots)
        rows[CAP:, :] = jnp.zeros((WINDOW, rows.shape[1]), bf16)
        firsts = [f_low[i] for i in range(3)] + [f_high[i] for i in range(3)]
        thirds = [t_low[0], t_high[0]]
        weight = whole_block((here, there), 2, offs_ref[depth_ref.shape[0] + 1])
        for half in range(2):
            at = slice(half * HALF, (half + 1) * HALF)
            pieces = [firsts[2 * head + half] for head in range(3)] + [thirds[half], last[half]]
            rows[at, :] = (near[at, :] + group_term(pieces, weight, cbuf)).astype(bf16)

    def body(sub, carry):
        block = step * STEP_BLOCKS + sub
        at = pl.multiple_of(sub * TOK_BLOCK, TOK_BLOCK)

        def run(start, shift_by, window):
            spread = lax.dot_general(
                window_onehot(slots, block, shift_by, window),
                rows[pl.ds(start, window), :],
                (((0,), (0,)), ((), ())),
                preferred_element_type=f32,
            )
            out[pl.ds(at, TOK_BLOCK), :] = spread.astype(bf16)

        by_window(offs_ref, block, run)
        return carry

    lax.fori_loop(0, STEP_BLOCKS, body, 0)


def output_update(offsets, depth_blocks, pieces, gathered, near, length):
    width = near.shape[1]
    blocks = length // TOK_BLOCK
    rows = STEP_BLOCKS * TOK_BLOCK

    operands = (depth_blocks, *pieces, *gathered, near)
    return pl.pallas_call(
        output_kernel,
        out_shape=jax.ShapeDtypeStruct((length, width), bf16),
        grid_spec=pltpu.PrefetchScalarGridSpec(
            num_scalar_prefetch=1,
            grid=(length // rows,),
            in_specs=vmem_specs(len(operands)),
            out_specs=pl.BlockSpec((rows, width), lambda i, o: (i, 0)),
            scratch_shapes=[
                pltpu.VMEM((HALF, 5 * HD), bf16),
                pltpu.VMEM((ROOM, width), bf16),
                pltpu.VMEM((blocks, TOK_BLOCK), jnp.int32),
            ],
        ),
        compiler_params=params(16),
        cost_estimate=cost(8),
        name="output",
    )(offsets, *operands)


def shift(value, axis, distance):
    size = lax.axis_size(axis)
    return lax.ppermute(value, axis, [(i, (i + distance) % size) for i in range(size)])


def swap(value, axis, bit):
    return lax.ppermute(value, axis, [(i, i ^ bit) for i in range(lax.axis_size(axis))])


def after(value, *others):
    return lax.optimization_barrier((value, others))[0]


def ring_near(value):
    return [shift(value, "tensor", 1), shift(value, "tensor", -1)]


def ring_far(near):
    middle = near[0].shape[0] // 2
    return [shift(near[0][:middle], "tensor", 1), shift(near[1][middle:], "tensor", -1)]


def per_device(hidden, depth, qkv_weight, out_weight):
    tokens = hidden[0]
    length, width = tokens.shape
    t = lax.axis_index("tensor")
    ctx = lax.axis_index("ctx")
    depth_blocks = depth.reshape(length // TOK_BLOCK, TOK_BLOCK)
    block_counts = jnp.sum((depth_blocks >= RECURSION).astype(jnp.int32), axis=1)
    ends = jnp.arange(length // TOK_BLOCK + 1)
    offsets = jnp.sum(
        jnp.where(ends[:, None] > ends[None, :-1], block_counts[None, :], 0), axis=1
    ).astype(jnp.int32)
    count = jnp.sum(block_counts).reshape(1)
    place_both = jnp.stack([t, ctx]).astype(jnp.int32)
    weight = jnp.transpose(qkv_weight, (1, 0, 2))

    x0, x1, squares = compact_rows(tokens, depth_blocks, offsets)
    squares = sum([squares] + [shift(squares, "tensor", d) for d in (1, 2, 3)])
    squares0, squares1 = squares[:, :HALF], squares[:, HALF:]


    def column_block(rows, distance):
        start = ((t + distance) & 3) * width
        return lax.dynamic_slice_in_dim(rows, start, width, axis=rows.ndim - 1)

    own_block = column_block(out_weight, 0)
    dp = lax.axis_index("dp")
    shares = out_weight.reshape(5, SHARES, HD // SHARES, out_weight.shape[1])
    shares = lax.dynamic_slice_in_dim(shares, dp & (SHARES - 1), 1, axis=1)[:, 0]
    turned = lax.dynamic_slice_in_dim(jnp.concatenate([shares[:4], shares[:4]]), ctx, 4)
    shares = jnp.concatenate([turned, shares[4:]])

    near0 = ring_near(x0)
    count = after(count, near0)
    others = [shift(count, "ctx", s) for s in (1, 2, 3)]
    far0 = ring_far(near0)
    near_sum = project_near(place_both, squares0, x0, *near0, weight)
    x1, others = after((x1, others), far0, near_sum)
    place_ctx = jnp.stack([ctx.astype(jnp.int32), count[0], *[o[0] for o in others], dp.astype(jnp.int32)])
    near1 = ring_near(x1)
    first = project(place_both, squares0, near_sum, *far0, weight)
    sent0 = [first[0]] + [shift(first[s], "ctx", s) for s in (1, 2, 3)]
    far1 = ring_far(after(near1, first))
    near_sum = project_near(place_both, squares1, x1, *near1, weight)
    second = project(place_both, squares1, near_sum, *far1, weight)
    second, shares = after((second, shares), sent0)
    moved = [shift(column_block(shares, d), "tensor", d) for d in (1, 3, 2)]
    gathered = jnp.stack(moved)[None]
    gathered = jnp.concatenate([gathered, swap(gathered, "dp", 2)])
    gathered = (gathered, swap(gathered, "dp", 1))
    sent1 = [second[0]] + [shift(second[s], "ctx", s) for s in (1, 2, 3)]
    arrived = [piece for s in range(4) for piece in (sent0[s], sent1[s])]

    last = attend_last(place_ctx, (first[4], second[4]), arrived)
    lasts = [last] + ring_near(last) + [shift(last, "tensor", 2)]
    to_near, to_far = attend_main(1, after(place_ctx, last), arrived)
    back = [shift(to_near, "ctx", -1), shift(to_far, "ctx", -2)]
    to_right, own = attend_main(3, after(place_ctx, to_near, to_far, lasts), arrived)
    back.append(shift(to_right, "ctx", -3))
    own, lasts, gathered = lax.optimization_barrier((own, lasts, gathered))
    firsts = jnp.concatenate([own, back[0], back[1]])
    near = ring_near(firsts)
    third = after(back[2], near)
    firsts = [firsts] + near + ring_far(near)
    near = ring_near(third)
    thirds = [third] + near + ring_far(near)
    summed = near_terms(place_ctx, lasts[:3], firsts[:3], thirds[:3], own_block, gathered)
    pieces = [lasts[3]] + firsts[3:] + thirds[3:]
    update = output_update(
        jnp.concatenate([offsets, dp.reshape(1).astype(jnp.int32)]),
        depth_blocks,
        pieces,
        gathered,
        summed,
        length,
    )
    return update[None]


def solution(mesh):
    placed = (P("dp", "ctx", "tensor"), P("dp", "ctx"), P(None, None, "tensor"), P("tensor", None))
    return jax.shard_map(
        per_device, mesh=mesh, in_specs=placed, out_specs=P("dp", "ctx", "tensor"), check_vma=False
    )
```

```python
import functools
import math

import jax
import jax.numpy as jnp
from jax import lax
from jax.experimental import pallas as pl
from jax.experimental.pallas import tpu as pltpu
from jax.sharding import PartitionSpec as P

HD = 128
RECURSION = 3
CAP = 1024
HALF = CAP // 2
SUB = CAP // 4
TOK_BLOCK = 256
WINDOW = TOK_BLOCK + 16
SMALL = 128
STEP_BLOCKS = 4
SHARES = 4
ROOM = CAP + WINDOW

score_scale = 0.25
norm_epsilon = 1e-05
head_epsilon = 1e-06
EXP2_SCALE = score_scale / math.log(2.0)
MEBI = 1024 * 1024

bf16 = jnp.bfloat16
f32 = jnp.float32


def cost(micros):
    return pl.CostEstimate(flops=int(micros * 1.1e9), bytes_accessed=0, transcendentals=0)


def params(mebibytes):
    return pltpu.CompilerParams(vmem_limit_bytes=mebibytes * MEBI)


def in_hbm(value):
    return pltpu.with_memory_space_constraint(value, pltpu.HBM)


def fill_slots(depth_ref, slots):
    active = depth_ref[...] >= RECURSION
    flags = jnp.where(active, 1.0, 0.0).astype(bf16)
    before = lax.broadcasted_iota(jnp.int32, (TOK_BLOCK, TOK_BLOCK), 0)
    after_it = lax.broadcasted_iota(jnp.int32, (TOK_BLOCK, TOK_BLOCK), 1)
    earlier = jnp.where(before < after_it, 1.0, 0.0).astype(bf16)
    rank = jnp.dot(flags, earlier, preferred_element_type=f32).astype(jnp.int32)
    slots[...] = jnp.where(active, rank, -2 * CAP)


def window_onehot(slots, block, shift_by, window):
    rows = lax.broadcasted_iota(jnp.int32, (window, TOK_BLOCK), 0)
    return jnp.where(rows == slots[pl.ds(block, 1), :] + shift_by, 1.0, 0.0).astype(bf16)


def by_window(offs_ref, block, run):
    low, high = offs_ref[block], offs_ref[block + 1]
    start = pl.multiple_of((low >> 4) << 4, 16)

    @pl.when(high - start <= SMALL)
    def _():
        run(start, low - start, SMALL)

    @pl.when(high - start > SMALL)
    def _():
        run(start, low - start, WINDOW)


def compact_kernel(offs_ref, depth_ref, tok_ref, o0, o1, buf, slots):
    step = pl.program_id(0)

    @pl.when(step == 0)
    def _():
        buf[...] = jnp.zeros_like(buf)
        fill_slots(depth_ref, slots)

    def body(sub, carry):
        block = step * STEP_BLOCKS + sub
        at = pl.multiple_of(sub * TOK_BLOCK, TOK_BLOCK)

        def run(start, shift_by, window):
            picked = jnp.dot(
                window_onehot(slots, block, shift_by, window),
                tok_ref[pl.ds(at, TOK_BLOCK), :],
                preferred_element_type=f32,
            ).astype(bf16)
            buf[pl.ds(start, window), :] = buf[pl.ds(start, window), :] + picked

        by_window(offs_ref, block, run)
        return carry

    lax.fori_loop(0, STEP_BLOCKS, body, 0)

    @pl.when(step == pl.num_programs(0) - 1)
    def _():
        for i, o in enumerate((o0, o1)):
            o[...] = buf[i * HALF : (i + 1) * HALF, :]


def compact_rows(tokens, depth_blocks, offsets):
    length, width = tokens.shape
    blocks = length // TOK_BLOCK
    rows = STEP_BLOCKS * TOK_BLOCK
    return pl.pallas_call(
        compact_kernel,
        out_shape=(jax.ShapeDtypeStruct((HALF, width), bf16),) * 2,
        grid_spec=pltpu.PrefetchScalarGridSpec(
            num_scalar_prefetch=1,
            grid=(length // rows,),
            in_specs=[
                pl.BlockSpec((blocks, TOK_BLOCK), lambda i, o: (0, 0)),
                pl.BlockSpec((rows, width), lambda i, o: (i, 0)),
            ],
            out_specs=(pl.BlockSpec((HALF, width), lambda i, o: (0, 0)),) * 2,
            scratch_shapes=[
                pltpu.VMEM((ROOM, width), bf16),
                pltpu.VMEM((blocks, TOK_BLOCK), jnp.int32),
            ],
        ),
        compiler_params=params(12),
        cost_estimate=cost(8),
        name="compact",
    )(offsets, depth_blocks, in_hbm(tokens))


def project_kernel(place, x, a, b, c, d, w_hbm, o0, o1, o2, o3, q4, xs, acc, w_ref, sems):
    t = place[0]
    ctx = place[1]
    copies = [
        pltpu.make_async_copy(w_hbm.at[part], w_ref.at[part], sems.at[part]) for part in range(3)
    ]
    for copy in copies:
        copy.start()
    width = x.shape[1]
    for sub, far in enumerate((c, d)):
        low = sub * SUB
        pieces = [p[low : low + SUB, :] for p in (x, a, b)] + [far[...]]
        squares = jnp.zeros((SUB, 1), f32)
        for piece in pieces:
            wide = piece.astype(f32)
            squares = squares + jnp.sum(wide * wide, axis=1, keepdims=True)
        factor = lax.rsqrt(squares * (1.0 / (4 * width)) + norm_epsilon)
        for distance, piece in zip((0, 3, 1, 2), pieces):
            lane = pl.multiple_of(((t + distance) & 3) * width, 128)
            normed = (piece.astype(f32) * factor).astype(bf16)
            xs[low : low + SUB, pl.ds(lane, width)] = normed

    outs = (o0, o1, o2, o3)
    for part in range(3):
        copies[part].wait()
        acc[part] = jnp.dot(xs[...], w_ref[part], preferred_element_type=f32)

        def column(y):
            if part == 2:
                return y.astype(bf16)
            scale = lax.rsqrt(jnp.mean(y * y, axis=1, keepdims=True) + head_epsilon)
            return (y * scale).astype(bf16)

        for slot, out in enumerate(outs):
            lane = pl.multiple_of(((ctx + slot) & 3) * HD, HD)
            out[part] = column(acc[part, :, pl.ds(lane, HD)])
        z = column(acc[part, :, 4 * HD : 5 * HD])
        if part == 0:
            q4[...] = z
        else:
            for out in outs:
                out[part + 2] = z


def project(place, own, left, right, far_low, far_high, weight, micros):
    width = own.shape[1]
    return pl.pallas_call(
        project_kernel,
        out_shape=(jax.ShapeDtypeStruct((5, HALF, HD), bf16),) * 4
        + (jax.ShapeDtypeStruct((HALF, HD), bf16),),
        in_specs=[pl.BlockSpec(memory_space=pltpu.SMEM)]
        + vmem_specs(5)
        + [pl.BlockSpec(memory_space=pltpu.HBM)],
        out_specs=tuple(vmem_specs(5)),
        scratch_shapes=[
            pltpu.VMEM((HALF, 4 * width), bf16),
            pltpu.VMEM((3, HALF, 5 * HD), f32),
            pltpu.VMEM(weight.shape, bf16),
            pltpu.SemaphoreType.DMA((3,)),
        ],
        compiler_params=params(28),
        cost_estimate=cost(micros),
        name="project",
    )(place, own, left, right, far_low, far_high, in_hbm(weight))


def attend_block(block, count, query, count_of, ks, vs, acc):
    def add_tiles(chunk, base=None):
        scores = [
            jnp.dot(query[at : at + HALF, :], ks[chunk], preferred_element_type=f32)
            for at in (0, HALF)
        ]
        for at, score in zip((0, HALF), scores):
            weights = jnp.exp2(score * EXP2_SCALE)
            if base is not None:
                row = lax.broadcasted_iota(jnp.int32, (HALF, HALF), 0) + (at - base)
                col = lax.broadcasted_iota(jnp.int32, (HALF, HALF), 1)
                weights = jnp.where(col <= row, weights, 0.0)
            acc[at : at + HALF, :] += jnp.dot(
                weights.astype(bf16), vs[chunk], preferred_element_type=f32
            )

    acc[...] = jnp.zeros_like(acc)

    @pl.when(count > 0)
    def _():
        def earlier(chunk, carry):
            @pl.when(count_of(chunk >> 1) > (chunk & 1) * HALF)
            def _():
                add_tiles(chunk)

            return carry

        def same(half, carry):
            @pl.when(count > half * HALF)
            def _():
                add_tiles(2 * block + half, half * HALF)

            return carry

        lax.fori_loop(0, 2 * block, earlier, 0)
        lax.fori_loop(0, 2, same, 0)


def context_of(acc, low):
    total = acc[low : low + HALF, HD:]
    return (acc[low : low + HALF, :HD] / jnp.where(total == 0.0, 1.0, total)).astype(bf16)


def place_keys(chunk, half, count, key, value, ks, vs):
    @pl.when(count > half * HALF)
    def _():
        ks[chunk] = key.T
        rows = lax.broadcasted_iota(jnp.int32, (HALF, HD), 0) + half * HALF
        vs[chunk, :, :HD] = value
        vs[chunk, :, HD:] = jnp.where(rows < count, 1.0, 0.0).astype(bf16)


def attend_main_kernel(first_slot, place, *refs):
    inputs, outs, (qs, ks, vs, cs, acc) = refs[:8], refs[8:10], refs[10:]
    ctx = place[0]

    def count_of(block):
        return place[1 + ((ctx - block) & 3)]

    for s in range(4):
        block = (ctx - s) & 3
        for half in range(2):
            source = inputs[2 * s + half]
            qs[s, half * HALF : (half + 1) * HALF] = source[0]
            place_keys(2 * block + half, half, place[1 + s], source[1], source[2], ks, vs)

    def body(i, carry):
        s = (first_slot + i) & 3
        attend_block((ctx - s) & 3, place[1 + s], qs.at[s], count_of, ks, vs, acc)
        for half in range(2):
            cs[i, half] = context_of(acc, half * HALF)
        return carry

    lax.fori_loop(0, 2, body, 0)
    for i, out in enumerate(outs):
        out[...] = cs[i]


def vmem_specs(count):
    return [pl.BlockSpec(memory_space=pltpu.VMEM)] * count


def attend_main(first_slot, place, inputs):
    return pl.pallas_call(
        functools.partial(attend_main_kernel, first_slot),
        out_shape=(jax.ShapeDtypeStruct((2, HALF, HD), bf16),) * 2,
        in_specs=[pl.BlockSpec(memory_space=pltpu.SMEM)] + vmem_specs(8),
        out_specs=tuple(vmem_specs(2)),
        scratch_shapes=[
            pltpu.VMEM((4, CAP, HD), bf16),
            pltpu.VMEM((8, HD, HALF), bf16),
            pltpu.VMEM((8, HALF, 2 * HD), bf16),
            pltpu.VMEM((2, 2, HALF, HD), bf16),
            pltpu.VMEM((CAP, 2 * HD), f32),
        ],
        compiler_params=params(16),
        cost_estimate=cost(10),
        name="attend_main",
    )(place, *inputs)


def attend_last_kernel(place, q0, q1, *refs):
    inputs, (out, qs, ks, vs, acc) = refs[:8], refs[8:]
    ctx = place[0]

    def count_of(block):
        return place[1 + ((ctx - block) & 3)]

    for s in range(4):

        @pl.when(s <= ctx)
        def _():
            for half in range(2):
                source = inputs[2 * s + half]
                chunk = (ctx - s) * 2 + half
                place_keys(chunk, half, place[1 + s], source[3], source[4], ks, vs)

    qs[:HALF, :] = q0[...]
    qs[HALF:, :] = q1[...]
    attend_block(ctx, place[1], qs, count_of, ks, vs, acc)
    for half in range(2):
        out[half] = context_of(acc, half * HALF)


def attend_last(place, queries, inputs):
    return pl.pallas_call(
        attend_last_kernel,
        out_shape=jax.ShapeDtypeStruct((2, HALF, HD), bf16),
        in_specs=[pl.BlockSpec(memory_space=pltpu.SMEM)] + vmem_specs(10),
        out_specs=vmem_specs(1)[0],
        scratch_shapes=[
            pltpu.VMEM((CAP, HD), bf16),
            pltpu.VMEM((8, HD, HALF), bf16),
            pltpu.VMEM((8, HALF, 2 * HD), bf16),
            pltpu.VMEM((CAP, 2 * HD), f32),
        ],
        compiler_params=params(16),
        cost_estimate=cost(4),
        name="attend_last",
    )(place, *queries, *inputs)


def group_term(pieces, weight, cbuf):
    for i, piece in enumerate(pieces):
        cbuf[:, i * HD : (i + 1) * HD] = piece
    term = jnp.dot(cbuf[...], weight, preferred_element_type=f32)
    return term.astype(bf16).astype(f32)


def whole_block(gathered, which, dp):
    places = []
    for share in range(SHARES):
        other = (dp & (SHARES - 1)) ^ share
        places.append((other >> 1, (other & 1) == 1))
    here, there = gathered
    parts = [
        jnp.where(swapped, there[place, which, slot], here[place, which, slot])
        for slot in range(5)
        for place, swapped in places
    ]
    return jnp.concatenate(parts, axis=0)


def near_terms_kernel(place, *refs):
    lasts, firsts, thirds, (own, *gathered), (out, cbuf, held) = (
        refs[:3],
        refs[3:6],
        refs[6:9],
        refs[9:12],
        refs[12:],
    )
    for source, (last, first, third) in enumerate(zip(lasts, firsts, thirds)):
        if source == 0:
            starts = [pl.multiple_of(((place[0] + slot) & 3) * HD, HD) for slot in range(4)]
            parts = [own[pl.ds(start, HD), :] for start in starts]
            weight = jnp.concatenate(parts + [own[4 * HD :, :]], axis=0)
        else:
            weight = whole_block(gathered, source - 1, place[5])
        held[...] = weight

        def body(half, carry):
            at = pl.ds(pl.multiple_of(half * HALF, HALF), HALF)
            pieces = [first[2 * head + half] for head in range(3)] + [third[half], last[half]]
            term = group_term(pieces, held[...], cbuf)
            out[at, :] = term if source == 0 else out[at, :] + term
            return carry

        lax.fori_loop(0, 2, body, 0)


def near_terms(place, lasts, firsts, thirds, own_block, gathered):
    return pl.pallas_call(
        near_terms_kernel,
        out_shape=jax.ShapeDtypeStruct((CAP, own_block.shape[1]), f32),
        in_specs=[pl.BlockSpec(memory_space=pltpu.SMEM)] + vmem_specs(12),
        out_specs=vmem_specs(1)[0],
        scratch_shapes=[
            pltpu.VMEM((HALF, 5 * HD), bf16),
            pltpu.VMEM(own_block.shape, bf16),
        ],
        compiler_params=params(12),
        cost_estimate=cost(5),
        name="near_terms",
    )(place, *lasts, *firsts, *thirds, own_block, *gathered)


def output_kernel(offs_ref, depth_ref, last, f_low, f_high, t_low, t_high, here, there, near, out, *scratch):
    cbuf, rows, slots = scratch
    step = pl.program_id(0)

    @pl.when(step == 0)
    def _():
        fill_slots(depth_ref, slots)
        rows[CAP:, :] = jnp.zeros((WINDOW, rows.shape[1]), bf16)
        firsts = [f_low[i] for i in range(3)] + [f_high[i] for i in range(3)]
        thirds = [t_low[0], t_high[0]]
        weight = whole_block((here, there), 2, offs_ref[depth_ref.shape[0] + 1])
        for half in range(2):
            at = slice(half * HALF, (half + 1) * HALF)
            pieces = [firsts[2 * head + half] for head in range(3)] + [thirds[half], last[half]]
            rows[at, :] = (near[at, :] + group_term(pieces, weight, cbuf)).astype(bf16)

    def body(sub, carry):
        block = step * STEP_BLOCKS + sub
        at = pl.multiple_of(sub * TOK_BLOCK, TOK_BLOCK)

        def run(start, shift_by, window):
            spread = lax.dot_general(
                window_onehot(slots, block, shift_by, window),
                rows[pl.ds(start, window), :],
                (((0,), (0,)), ((), ())),
                preferred_element_type=f32,
            )
            out[pl.ds(at, TOK_BLOCK), :] = spread.astype(bf16)

        by_window(offs_ref, block, run)
        return carry

    lax.fori_loop(0, STEP_BLOCKS, body, 0)


def output_update(offsets, depth_blocks, pieces, gathered, near, length):
    width = near.shape[1]
    blocks = length // TOK_BLOCK
    rows = STEP_BLOCKS * TOK_BLOCK

    operands = (depth_blocks, *pieces, *gathered, near)
    return pl.pallas_call(
        output_kernel,
        out_shape=jax.ShapeDtypeStruct((length, width), bf16),
        grid_spec=pltpu.PrefetchScalarGridSpec(
            num_scalar_prefetch=1,
            grid=(length // rows,),
            in_specs=vmem_specs(len(operands)),
            out_specs=pl.BlockSpec((rows, width), lambda i, o: (i, 0)),
            scratch_shapes=[
                pltpu.VMEM((HALF, 5 * HD), bf16),
                pltpu.VMEM((ROOM, width), bf16),
                pltpu.VMEM((blocks, TOK_BLOCK), jnp.int32),
            ],
        ),
        compiler_params=params(16),
        cost_estimate=cost(8),
        name="output",
    )(offsets, *operands)


def shift(value, axis, distance):
    size = lax.axis_size(axis)
    return lax.ppermute(value, axis, [(i, (i + distance) % size) for i in range(size)])


def swap(value, axis, bit):
    return lax.ppermute(value, axis, [(i, i ^ bit) for i in range(lax.axis_size(axis))])


def after(value, *others):
    return lax.optimization_barrier((value, others))[0]


def ring_near(value):
    return [shift(value, "tensor", 1), shift(value, "tensor", -1)]


def ring_far(near):
    middle = near[0].shape[0] // 2
    return [shift(near[0][:middle], "tensor", 1), shift(near[1][middle:], "tensor", -1)]


def per_device(hidden, depth, qkv_weight, out_weight):
    tokens = hidden[0]
    length, width = tokens.shape
    t = lax.axis_index("tensor")
    ctx = lax.axis_index("ctx")
    depth_blocks = depth.reshape(length // TOK_BLOCK, TOK_BLOCK)
    block_counts = jnp.sum((depth_blocks >= RECURSION).astype(jnp.int32), axis=1)
    ends = jnp.arange(length // TOK_BLOCK + 1)
    offsets = jnp.sum(
        jnp.where(ends[:, None] > ends[None, :-1], block_counts[None, :], 0), axis=1
    ).astype(jnp.int32)
    count = jnp.sum(block_counts).reshape(1)
    place_both = jnp.stack([t, ctx]).astype(jnp.int32)
    weight = jnp.transpose(qkv_weight, (1, 0, 2))

    x0, x1 = compact_rows(tokens, depth_blocks, offsets)


    def column_block(rows, distance):
        start = ((t + distance) & 3) * width
        return lax.dynamic_slice_in_dim(rows, start, width, axis=rows.ndim - 1)

    own_block = column_block(out_weight, 0)
    dp = lax.axis_index("dp")
    shares = out_weight.reshape(5, SHARES, HD // SHARES, out_weight.shape[1])
    shares = lax.dynamic_slice_in_dim(shares, dp & (SHARES - 1), 1, axis=1)[:, 0]
    turned = lax.dynamic_slice_in_dim(jnp.concatenate([shares[:4], shares[:4]]), ctx, 4)
    shares = jnp.concatenate([turned, shares[4:]])

    near0 = ring_near(x0)
    count = after(count, near0)
    others = [shift(count, "ctx", s) for s in (1, 2, 3)]
    far0 = ring_far(near0)
    x1, others = after((x1, others), far0)
    place_ctx = jnp.stack([ctx.astype(jnp.int32), count[0], *[o[0] for o in others], dp.astype(jnp.int32)])
    near1 = ring_near(x1)
    first = project(place_both, x0, *near0, *far0, weight, 9)
    sent0 = [first[0]] + [shift(first[s], "ctx", s) for s in (1, 2, 3)]
    far1 = ring_far(after(near1, first))
    second = project(place_both, x1, *near1, *far1, weight, 9)
    second, shares = after((second, shares), sent0)
    moved = [shift(column_block(shares, d), "tensor", d) for d in (1, 3, 2)]
    gathered = jnp.stack(moved)[None]
    gathered = jnp.concatenate([gathered, swap(gathered, "dp", 2)])
    gathered = (gathered, swap(gathered, "dp", 1))
    sent1 = [second[0]] + [shift(second[s], "ctx", s) for s in (1, 2, 3)]
    arrived = [piece for s in range(4) for piece in (sent0[s], sent1[s])]

    last = attend_last(place_ctx, (first[4], second[4]), arrived)
    lasts = [last] + ring_near(last) + [shift(last, "tensor", 2)]
    to_near, to_far = attend_main(1, after(place_ctx, last), arrived)
    back = [shift(to_near, "ctx", -1), shift(to_far, "ctx", -2)]
    to_right, own = attend_main(3, after(place_ctx, to_near, to_far, lasts), arrived)
    back.append(shift(to_right, "ctx", -3))
    own, lasts, gathered = lax.optimization_barrier((own, lasts, gathered))
    firsts = jnp.concatenate([own, back[0], back[1]])
    near = ring_near(firsts)
    third = after(back[2], near)
    firsts = [firsts] + near + ring_far(near)
    near = ring_near(third)
    thirds = [third] + near + ring_far(near)
    summed = near_terms(place_ctx, lasts[:3], firsts[:3], thirds[:3], own_block, gathered)
    pieces = [lasts[3]] + firsts[3:] + thirds[3:]
    update = output_update(
        jnp.concatenate([offsets, dp.reshape(1).astype(jnp.int32)]),
        depth_blocks,
        pieces,
        gathered,
        summed,
        length,
    )
    return update[None]


def solution(mesh):
    placed = (P("dp", "ctx", "tensor"), P("dp", "ctx"), P(None, None, "tensor"), P("tensor", None))
    return jax.shard_map(
        per_device, mesh=mesh, in_specs=placed, out_specs=P("dp", "ctx", "tensor"), check_vma=False
    )
```

```python
import functools
import math

import jax
import jax.numpy as jnp
from jax import lax
from jax.experimental import pallas as pl
from jax.experimental.pallas import tpu as pltpu
from jax.sharding import PartitionSpec as P

HD = 128
RECURSION = 3
CAP = 1024
HALF = CAP // 2
SUB = CAP // 4
TOK_BLOCK = 256
WINDOW = TOK_BLOCK + 16
SMALL = 128
STEP_BLOCKS = 4
SHARES = 4
ROOM = CAP + WINDOW

score_scale = 0.25
norm_epsilon = 1e-05
head_epsilon = 1e-06
EXP2_SCALE = score_scale / math.log(2.0)
MEBI = 1024 * 1024

bf16 = jnp.bfloat16
f32 = jnp.float32


def cost(micros):
    return pl.CostEstimate(flops=int(micros * 1.1e9), bytes_accessed=0, transcendentals=0)


def params(mebibytes):
    return pltpu.CompilerParams(vmem_limit_bytes=mebibytes * MEBI)


def in_hbm(value):
    return pltpu.with_memory_space_constraint(value, pltpu.HBM)


def fill_slots(depth_ref, slots):
    active = depth_ref[...] >= RECURSION
    flags = jnp.where(active, 1.0, 0.0).astype(bf16)
    before = lax.broadcasted_iota(jnp.int32, (TOK_BLOCK, TOK_BLOCK), 0)
    after_it = lax.broadcasted_iota(jnp.int32, (TOK_BLOCK, TOK_BLOCK), 1)
    earlier = jnp.where(before < after_it, 1.0, 0.0).astype(bf16)
    rank = jnp.dot(flags, earlier, preferred_element_type=f32).astype(jnp.int32)
    slots[...] = jnp.where(active, rank, -2 * CAP)


def window_onehot(slots, block, shift_by, window):
    rows = lax.broadcasted_iota(jnp.int32, (window, TOK_BLOCK), 0)
    return jnp.where(rows == slots[pl.ds(block, 1), :] + shift_by, 1.0, 0.0).astype(bf16)


def by_window(offs_ref, block, run):
    low, high = offs_ref[block], offs_ref[block + 1]
    start = pl.multiple_of((low >> 4) << 4, 16)

    @pl.when(high - start <= SMALL)
    def _():
        run(start, low - start, SMALL)

    @pl.when(high - start > SMALL)
    def _():
        run(start, low - start, WINDOW)


def compact_kernel(offs_ref, depth_ref, tok_ref, o0, o1, buf, slots):
    step = pl.program_id(0)

    @pl.when(step == 0)
    def _():
        buf[...] = jnp.zeros_like(buf)
        fill_slots(depth_ref, slots)

    def body(sub, carry):
        block = step * STEP_BLOCKS + sub
        at = pl.multiple_of(sub * TOK_BLOCK, TOK_BLOCK)

        def run(start, shift_by, window):
            picked = jnp.dot(
                window_onehot(slots, block, shift_by, window),
                tok_ref[pl.ds(at, TOK_BLOCK), :],
                preferred_element_type=f32,
            ).astype(bf16)
            buf[pl.ds(start, window), :] = buf[pl.ds(start, window), :] + picked

        by_window(offs_ref, block, run)
        return carry

    lax.fori_loop(0, STEP_BLOCKS, body, 0)

    @pl.when(step == pl.num_programs(0) - 1)
    def _():
        for i, o in enumerate((o0, o1)):
            o[...] = buf[i * HALF : (i + 1) * HALF, :]


def compact_rows(tokens, depth_blocks, offsets):
    length, width = tokens.shape
    blocks = length // TOK_BLOCK
    rows = STEP_BLOCKS * TOK_BLOCK
    return pl.pallas_call(
        compact_kernel,
        out_shape=(jax.ShapeDtypeStruct((HALF, width), bf16),) * 2,
        grid_spec=pltpu.PrefetchScalarGridSpec(
            num_scalar_prefetch=1,
            grid=(length // rows,),
            in_specs=[
                pl.BlockSpec((blocks, TOK_BLOCK), lambda i, o: (0, 0)),
                pl.BlockSpec((rows, width), lambda i, o: (i, 0)),
            ],
            out_specs=(pl.BlockSpec((HALF, width), lambda i, o: (0, 0)),) * 2,
            scratch_shapes=[
                pltpu.VMEM((ROOM, width), bf16),
                pltpu.VMEM((blocks, TOK_BLOCK), jnp.int32),
            ],
        ),
        compiler_params=params(12),
        cost_estimate=cost(8),
        name="compact",
    )(offsets, depth_blocks, in_hbm(tokens))


def project_kernel(place, x, a, b, c, d, w_hbm, o0, o1, o2, o3, q4, xs, acc, w_ref, sems):
    t = place[0]
    ctx = place[1]
    copies = [
        pltpu.make_async_copy(w_hbm.at[part], w_ref.at[part], sems.at[part]) for part in range(3)
    ]
    for copy in copies:
        copy.start()
    width = x.shape[1]
    for sub, far in enumerate((c, d)):
        low = sub * SUB
        pieces = [p[low : low + SUB, :] for p in (x, a, b)] + [far[...]]
        squares = jnp.zeros((SUB, 1), f32)
        for piece in pieces:
            wide = piece.astype(f32)
            squares = squares + jnp.sum(wide * wide, axis=1, keepdims=True)
        factor = lax.rsqrt(squares * (1.0 / (4 * width)) + norm_epsilon)
        for distance, piece in zip((0, 3, 1, 2), pieces):
            lane = pl.multiple_of(((t + distance) & 3) * width, 128)
            normed = (piece.astype(f32) * factor).astype(bf16)
            xs[low : low + SUB, pl.ds(lane, width)] = normed

    outs = (o0, o1, o2, o3)
    for part in range(3):
        copies[part].wait()
        acc[part] = jnp.dot(xs[...], w_ref[part], preferred_element_type=f32)

        def column(y):
            if part == 2:
                return y.astype(bf16)
            scale = lax.rsqrt(jnp.mean(y * y, axis=1, keepdims=True) + head_epsilon)
            return (y * scale).astype(bf16)

        for slot, out in enumerate(outs):
            lane = pl.multiple_of(((ctx + slot) & 3) * HD, HD)
            out[part] = column(acc[part, :, pl.ds(lane, HD)])
        z = column(acc[part, :, 4 * HD : 5 * HD])
        if part == 0:
            q4[...] = z
        else:
            for out in outs:
                out[part + 2] = z


def project(place, own, left, right, far_low, far_high, weight, micros):
    width = own.shape[1]
    return pl.pallas_call(
        project_kernel,
        out_shape=(jax.ShapeDtypeStruct((5, HALF, HD), bf16),) * 4
        + (jax.ShapeDtypeStruct((HALF, HD), bf16),),
        in_specs=[pl.BlockSpec(memory_space=pltpu.SMEM)]
        + vmem_specs(5)
        + [pl.BlockSpec(memory_space=pltpu.HBM)],
        out_specs=tuple(vmem_specs(5)),
        scratch_shapes=[
            pltpu.VMEM((HALF, 4 * width), bf16),
            pltpu.VMEM((3, HALF, 5 * HD), f32),
            pltpu.VMEM(weight.shape, bf16),
            pltpu.SemaphoreType.DMA((3,)),
        ],
        compiler_params=params(28),
        cost_estimate=cost(micros),
        name="project",
    )(place, own, left, right, far_low, far_high, in_hbm(weight))


def attend_block(block, count, query, count_of, ks, vs, acc):
    def add_tiles(chunk, base=None):
        scores = [
            jnp.dot(query[at : at + HALF, :], ks[chunk], preferred_element_type=f32)
            for at in (0, HALF)
        ]
        for at, score in zip((0, HALF), scores):
            weights = jnp.exp2(score * EXP2_SCALE)
            if base is not None:
                row = lax.broadcasted_iota(jnp.int32, (HALF, HALF), 0) + (at - base)
                col = lax.broadcasted_iota(jnp.int32, (HALF, HALF), 1)
                weights = jnp.where(col <= row, weights, 0.0)
            acc[at : at + HALF, :] += jnp.dot(
                weights.astype(bf16), vs[chunk], preferred_element_type=f32
            )

    acc[...] = jnp.zeros_like(acc)

    @pl.when(count > 0)
    def _():
        def earlier(chunk, carry):
            @pl.when(count_of(chunk >> 1) > (chunk & 1) * HALF)
            def _():
                add_tiles(chunk)

            return carry

        def same(half, carry):
            @pl.when(count > half * HALF)
            def _():
                add_tiles(2 * block + half, half * HALF)

            return carry

        lax.fori_loop(0, 2 * block, earlier, 0)
        lax.fori_loop(0, 2, same, 0)


def context_of(acc, low):
    total = acc[low : low + HALF, HD:]
    return (acc[low : low + HALF, :HD] / jnp.where(total == 0.0, 1.0, total)).astype(bf16)


def place_keys(chunk, half, count, key, value, ks, vs):
    @pl.when(count > half * HALF)
    def _():
        ks[chunk] = key.T
        rows = lax.broadcasted_iota(jnp.int32, (HALF, HD), 0) + half * HALF
        vs[chunk, :, :HD] = value
        vs[chunk, :, HD:] = jnp.where(rows < count, 1.0, 0.0).astype(bf16)


def attend_main_kernel(first_slot, place, *refs):
    inputs, outs, (qs, ks, vs, cs, acc) = refs[:8], refs[8:10], refs[10:]
    ctx = place[0]

    def count_of(block):
        return place[1 + ((ctx - block) & 3)]

    for s in range(4):
        block = (ctx - s) & 3
        for half in range(2):
            source = inputs[2 * s + half]
            qs[s, half * HALF : (half + 1) * HALF] = source[0]
            place_keys(2 * block + half, half, place[1 + s], source[1], source[2], ks, vs)

    def body(i, carry):
        s = (first_slot + i) & 3
        attend_block((ctx - s) & 3, place[1 + s], qs.at[s], count_of, ks, vs, acc)
        for half in range(2):
            cs[i, half] = context_of(acc, half * HALF)
        return carry

    lax.fori_loop(0, 2, body, 0)
    for i, out in enumerate(outs):
        out[...] = cs[i]


def vmem_specs(count):
    return [pl.BlockSpec(memory_space=pltpu.VMEM)] * count


def attend_main(first_slot, place, inputs):
    return pl.pallas_call(
        functools.partial(attend_main_kernel, first_slot),
        out_shape=(jax.ShapeDtypeStruct((2, HALF, HD), bf16),) * 2,
        in_specs=[pl.BlockSpec(memory_space=pltpu.SMEM)] + vmem_specs(8),
        out_specs=tuple(vmem_specs(2)),
        scratch_shapes=[
            pltpu.VMEM((4, CAP, HD), bf16),
            pltpu.VMEM((8, HD, HALF), bf16),
            pltpu.VMEM((8, HALF, 2 * HD), bf16),
            pltpu.VMEM((2, 2, HALF, HD), bf16),
            pltpu.VMEM((CAP, 2 * HD), f32),
        ],
        compiler_params=params(16),
        cost_estimate=cost(10),
        name="attend_main",
    )(place, *inputs)


def attend_last_kernel(place, *refs):
    inputs, queries, (out, qs, kv, ks, vs, acc, sems) = refs[:8], refs[8:10], refs[10:]
    ctx = place[0]
    copies = [
        pltpu.make_async_copy(source.at[pl.ds(3, 2)], kv.at[i], sems.at[i])
        for i, source in enumerate(inputs)
    ]
    copies += [
        pltpu.make_async_copy(query, qs.at[pl.ds(i * HALF, HALF)], sems.at[8 + i])
        for i, query in enumerate(queries)
    ]
    for copy in copies:
        copy.start()

    def count_of(block):
        return place[1 + ((ctx - block) & 3)]

    for copy in copies:
        copy.wait()
    for s in range(4):

        @pl.when(s <= ctx)
        def _():
            for half in range(2):
                source = kv.at[2 * s + half]
                chunk = (ctx - s) * 2 + half
                place_keys(chunk, half, place[1 + s], source[0], source[1], ks, vs)

    attend_block(ctx, place[1], qs, count_of, ks, vs, acc)
    for half in range(2):
        out[half] = context_of(acc, half * HALF)


def attend_last(place, queries, inputs):
    operands = [in_hbm(a) for a in (*inputs, *queries)]
    return pl.pallas_call(
        attend_last_kernel,
        out_shape=jax.ShapeDtypeStruct((2, HALF, HD), bf16),
        in_specs=[pl.BlockSpec(memory_space=pltpu.SMEM)]
        + [pl.BlockSpec(memory_space=pltpu.HBM)] * 10,
        out_specs=vmem_specs(1)[0],
        scratch_shapes=[
            pltpu.VMEM((CAP, HD), bf16),
            pltpu.VMEM((8, 2, HALF, HD), bf16),
            pltpu.VMEM((8, HD, HALF), bf16),
            pltpu.VMEM((8, HALF, 2 * HD), bf16),
            pltpu.VMEM((CAP, 2 * HD), f32),
            pltpu.SemaphoreType.DMA((10,)),
        ],
        compiler_params=params(16),
        cost_estimate=cost(4),
        name="attend_last",
    )(place, *operands)


def group_term(pieces, weight, cbuf):
    for i, piece in enumerate(pieces):
        cbuf[:, i * HD : (i + 1) * HD] = piece
    term = jnp.dot(cbuf[...], weight, preferred_element_type=f32)
    return term.astype(bf16).astype(f32)


def whole_block(gathered, which, dp):
    places = []
    for share in range(SHARES):
        other = (dp & (SHARES - 1)) ^ share
        places.append((other >> 1, (other & 1) == 1))
    here, there = gathered
    parts = [
        jnp.where(swapped, there[place, which, slot], here[place, which, slot])
        for slot in range(5)
        for place, swapped in places
    ]
    return jnp.concatenate(parts, axis=0)


def add_terms(out, held, cbuf, weight, pieces_of, before):
    held[...] = weight

    def body(half, carry):
        at = pl.ds(pl.multiple_of(half * HALF, HALF), HALF)
        term = group_term(pieces_of(half), held[...], cbuf)
        out[at, :] = term if before is None else before[at, :] + term
        return carry

    lax.fori_loop(0, 2, body, 0)


def pieces_of(first, third, last):
    return lambda half: [first[2 * head + half] for head in range(3)] + [third[half], last[half]]


def own_terms_kernel(place, last, first, third, own, out, cbuf, held):
    starts = [pl.multiple_of(((place[0] + slot) & 3) * HD, HD) for slot in range(4)]
    parts = [own[pl.ds(start, HD), :] for start in starts]
    weight = jnp.concatenate(parts + [own[4 * HD :, :]], axis=0)
    add_terms(out, held, cbuf, weight, pieces_of(first, third, last), None)


def near_terms_kernel(place, before, *refs):
    lasts, firsts, thirds, gathered, (out, cbuf, held) = (
        refs[:2],
        refs[2:4],
        refs[4:6],
        refs[6:8],
        refs[8:],
    )
    for i, (last, first, third) in enumerate(zip(lasts, firsts, thirds)):
        weight = whole_block(gathered, i, place[5])
        add_terms(
            out, held, cbuf, weight, pieces_of(first, third, last), before if i == 0 else out
        )


def terms_call(kernel, name, micros, place, width, operands):
    return pl.pallas_call(
        kernel,
        out_shape=jax.ShapeDtypeStruct((CAP, width), f32),
        in_specs=[pl.BlockSpec(memory_space=pltpu.SMEM)] + vmem_specs(len(operands)),
        out_specs=vmem_specs(1)[0],
        scratch_shapes=[
            pltpu.VMEM((HALF, 5 * HD), bf16),
            pltpu.VMEM((5 * HD, width), bf16),
        ],
        compiler_params=params(12),
        cost_estimate=cost(micros),
        name=name,
    )(place, *operands)


def output_kernel(offs_ref, depth_ref, last, f_low, f_high, t_low, t_high, here, there, near, out, *scratch):
    cbuf, rows, slots = scratch
    step = pl.program_id(0)

    @pl.when(step == 0)
    def _():
        fill_slots(depth_ref, slots)
        rows[CAP:, :] = jnp.zeros((WINDOW, rows.shape[1]), bf16)
        firsts = [f_low[i] for i in range(3)] + [f_high[i] for i in range(3)]
        thirds = [t_low[0], t_high[0]]
        weight = whole_block((here, there), 2, offs_ref[depth_ref.shape[0] + 1])
        for half in range(2):
            at = slice(half * HALF, (half + 1) * HALF)
            pieces = [firsts[2 * head + half] for head in range(3)] + [thirds[half], last[half]]
            rows[at, :] = (near[at, :] + group_term(pieces, weight, cbuf)).astype(bf16)

    def body(sub, carry):
        block = step * STEP_BLOCKS + sub
        at = pl.multiple_of(sub * TOK_BLOCK, TOK_BLOCK)

        def run(start, shift_by, window):
            spread = lax.dot_general(
                window_onehot(slots, block, shift_by, window),
                rows[pl.ds(start, window), :],
                (((0,), (0,)), ((), ())),
                preferred_element_type=f32,
            )
            out[pl.ds(at, TOK_BLOCK), :] = spread.astype(bf16)

        by_window(offs_ref, block, run)
        return carry

    lax.fori_loop(0, STEP_BLOCKS, body, 0)


def output_update(offsets, depth_blocks, pieces, gathered, near, length):
    width = near.shape[1]
    blocks = length // TOK_BLOCK
    rows = STEP_BLOCKS * TOK_BLOCK

    operands = (depth_blocks, *pieces, *gathered, near)
    return pl.pallas_call(
        output_kernel,
        out_shape=jax.ShapeDtypeStruct((length, width), bf16),
        grid_spec=pltpu.PrefetchScalarGridSpec(
            num_scalar_prefetch=1,
            grid=(length // rows,),
            in_specs=vmem_specs(len(operands)),
            out_specs=pl.BlockSpec((rows, width), lambda i, o: (i, 0)),
            scratch_shapes=[
                pltpu.VMEM((HALF, 5 * HD), bf16),
                pltpu.VMEM((ROOM, width), bf16),
                pltpu.VMEM((blocks, TOK_BLOCK), jnp.int32),
            ],
        ),
        compiler_params=params(16),
        cost_estimate=cost(8),
        name="output",
    )(offsets, *operands)


def shift(value, axis, distance):
    size = lax.axis_size(axis)
    return lax.ppermute(value, axis, [(i, (i + distance) % size) for i in range(size)])


def swap(value, axis, bit):
    return lax.ppermute(value, axis, [(i, i ^ bit) for i in range(lax.axis_size(axis))])


def after(value, *others):
    return lax.optimization_barrier((value, others))[0]


def ring_near(value):
    return [shift(value, "tensor", 1), shift(value, "tensor", -1)]


def ring_far(near):
    middle = near[0].shape[0] // 2
    return [shift(near[0][:middle], "tensor", 1), shift(near[1][middle:], "tensor", -1)]


def per_device(hidden, depth, qkv_weight, out_weight):
    tokens = hidden[0]
    length, width = tokens.shape
    t = lax.axis_index("tensor")
    ctx = lax.axis_index("ctx")
    depth_blocks = depth.reshape(length // TOK_BLOCK, TOK_BLOCK)
    block_counts = jnp.sum((depth_blocks >= RECURSION).astype(jnp.int32), axis=1)
    ends = jnp.arange(length // TOK_BLOCK + 1)
    offsets = jnp.sum(
        jnp.where(ends[:, None] > ends[None, :-1], block_counts[None, :], 0), axis=1
    ).astype(jnp.int32)
    count = jnp.sum(block_counts).reshape(1)
    place_both = jnp.stack([t, ctx]).astype(jnp.int32)
    weight = jnp.transpose(qkv_weight, (1, 0, 2))

    x0, x1 = compact_rows(tokens, depth_blocks, offsets)


    def column_block(rows, distance):
        start = ((t + distance) & 3) * width
        return lax.dynamic_slice_in_dim(rows, start, width, axis=rows.ndim - 1)

    own_block = column_block(out_weight, 0)
    dp = lax.axis_index("dp")
    shares = out_weight.reshape(5, SHARES, HD // SHARES, out_weight.shape[1])
    shares = lax.dynamic_slice_in_dim(shares, dp & (SHARES - 1), 1, axis=1)[:, 0]
    turned = lax.dynamic_slice_in_dim(jnp.concatenate([shares[:4], shares[:4]]), ctx, 4)
    shares = jnp.concatenate([turned, shares[4:]])

    near0 = ring_near(x0)
    count = after(count, near0)
    others = [shift(count, "ctx", s) for s in (1, 2, 3)]
    far0 = ring_far(near0)
    x1, others = after((x1, others), far0)
    place_ctx = jnp.stack([ctx.astype(jnp.int32), count[0], *[o[0] for o in others], dp.astype(jnp.int32)])
    near1 = ring_near(x1)
    first = project(place_both, x0, *near0, *far0, weight, 9)
    sent0 = [first[0]] + [shift(first[s], "ctx", s) for s in (1, 2, 3)]
    far1 = ring_far(after(near1, first))
    second = project(place_both, x1, *near1, *far1, weight, 9)
    second, shares = after((second, shares), sent0)
    moved = [shift(column_block(shares, d), "tensor", d) for d in (1, 3, 2)]
    gathered = jnp.stack(moved)[None]
    gathered = jnp.concatenate([gathered, swap(gathered, "dp", 2)])
    gathered = (gathered, swap(gathered, "dp", 1))
    sent1 = [second[0]] + [shift(second[s], "ctx", s) for s in (1, 2, 3)]
    arrived = [piece for s in range(4) for piece in (sent0[s], sent1[s])]

    last = attend_last(place_ctx, (first[4], second[4]), arrived)
    lasts = [last] + ring_near(last) + [shift(last, "tensor", 2)]
    to_near, to_far = attend_main(1, after(place_ctx, last), arrived)
    back = [shift(to_near, "ctx", -1), shift(to_far, "ctx", -2)]
    to_right, own = attend_main(3, after(place_ctx, to_near, to_far, lasts), arrived)
    back.append(shift(to_right, "ctx", -3))
    own, lasts, gathered = lax.optimization_barrier((own, lasts, gathered))
    firsts = jnp.concatenate([own, back[0], back[1]])
    near = ring_near(firsts)
    third = after(back[2], near)
    firsts = [firsts] + near + ring_far(near)
    near = ring_near(third)
    thirds = [third] + near + ring_far(near)
    operands = (lasts[0], firsts[0], thirds[0], own_block)
    summed = terms_call(own_terms_kernel, "own_terms", 2, place_ctx, width, operands)
    operands = (summed, *lasts[1:3], *firsts[1:3], *thirds[1:3], *gathered)
    summed = terms_call(near_terms_kernel, "near_terms", 4, place_ctx, width, operands)
    pieces = [lasts[3]] + firsts[3:] + thirds[3:]
    update = output_update(
        jnp.concatenate([offsets, dp.reshape(1).astype(jnp.int32)]),
        depth_blocks,
        pieces,
        gathered,
        summed,
        length,
    )
    return update[None]


def solution(mesh):
    placed = (P("dp", "ctx", "tensor"), P("dp", "ctx"), P(None, None, "tensor"), P("tensor", None))
    return jax.shard_map(
        per_device, mesh=mesh, in_specs=placed, out_specs=P("dp", "ctx", "tensor"), check_vma=False
    )
```

```python
import functools
import math

import jax
import jax.numpy as jnp
from jax import lax
from jax.experimental import pallas as pl
from jax.experimental.pallas import tpu as pltpu
from jax.sharding import PartitionSpec as P

HD = 128
RECURSION = 3
CAP = 1024
HALF = CAP // 2
SUB = CAP // 4
TOK_BLOCK = 256
WINDOW = TOK_BLOCK + 16
SMALL = 128
STEP_BLOCKS = 4
SHARES = 4
ROOM = CAP + WINDOW

score_scale = 0.25
norm_epsilon = 1e-05
head_epsilon = 1e-06
EXP2_SCALE = score_scale / math.log(2.0)
MEBI = 1024 * 1024

bf16 = jnp.bfloat16
f32 = jnp.float32


def cost(micros):
    return pl.CostEstimate(flops=int(micros * 1.1e9), bytes_accessed=0, transcendentals=0)


def params(mebibytes):
    return pltpu.CompilerParams(vmem_limit_bytes=mebibytes * MEBI)


def in_hbm(value):
    return pltpu.with_memory_space_constraint(value, pltpu.HBM)


def fill_slots(depth_ref, slots):
    active = depth_ref[...] >= RECURSION
    flags = jnp.where(active, 1.0, 0.0).astype(bf16)
    before = lax.broadcasted_iota(jnp.int32, (TOK_BLOCK, TOK_BLOCK), 0)
    after_it = lax.broadcasted_iota(jnp.int32, (TOK_BLOCK, TOK_BLOCK), 1)
    earlier = jnp.where(before < after_it, 1.0, 0.0).astype(bf16)
    rank = jnp.dot(flags, earlier, preferred_element_type=f32).astype(jnp.int32)
    slots[...] = jnp.where(active, rank, -2 * CAP)


def window_onehot(slots, block, shift_by, window):
    rows = lax.broadcasted_iota(jnp.int32, (window, TOK_BLOCK), 0)
    return jnp.where(rows == slots[pl.ds(block, 1), :] + shift_by, 1.0, 0.0).astype(bf16)


def by_window(offs_ref, block, run):
    low, high = offs_ref[block], offs_ref[block + 1]
    start = pl.multiple_of((low >> 4) << 4, 16)

    @pl.when(high - start <= SMALL)
    def _():
        run(start, low - start, SMALL)

    @pl.when(high - start > SMALL)
    def _():
        run(start, low - start, WINDOW)


def compact_kernel(offs_ref, depth_ref, tok_ref, o0, o1, buf, slots):
    step = pl.program_id(0)

    @pl.when(step == 0)
    def _():
        buf[...] = jnp.zeros_like(buf)
        fill_slots(depth_ref, slots)

    def body(sub, carry):
        block = step * STEP_BLOCKS + sub
        at = pl.multiple_of(sub * TOK_BLOCK, TOK_BLOCK)

        def run(start, shift_by, window):
            picked = jnp.dot(
                window_onehot(slots, block, shift_by, window),
                tok_ref[pl.ds(at, TOK_BLOCK), :],
                preferred_element_type=f32,
            ).astype(bf16)
            buf[pl.ds(start, window), :] = buf[pl.ds(start, window), :] + picked

        by_window(offs_ref, block, run)
        return carry

    lax.fori_loop(0, STEP_BLOCKS, body, 0)

    @pl.when(step == pl.num_programs(0) - 1)
    def _():
        for i, o in enumerate((o0, o1)):
            o[...] = buf[i * HALF : (i + 1) * HALF, :]


def compact_rows(tokens, depth_blocks, offsets):
    length, width = tokens.shape
    blocks = length // TOK_BLOCK
    rows = STEP_BLOCKS * TOK_BLOCK
    return pl.pallas_call(
        compact_kernel,
        out_shape=(jax.ShapeDtypeStruct((HALF, width), bf16),) * 2,
        grid_spec=pltpu.PrefetchScalarGridSpec(
            num_scalar_prefetch=1,
            grid=(length // rows,),
            in_specs=[
                pl.BlockSpec((blocks, TOK_BLOCK), lambda i, o: (0, 0)),
                pl.BlockSpec((rows, width), lambda i, o: (i, 0)),
            ],
            out_specs=(pl.BlockSpec((HALF, width), lambda i, o: (0, 0)),) * 2,
            scratch_shapes=[
                pltpu.VMEM((ROOM, width), bf16),
                pltpu.VMEM((blocks, TOK_BLOCK), jnp.int32),
            ],
        ),
        compiler_params=params(12),
        cost_estimate=cost(8),
        name="compact",
    )(offsets, depth_blocks, in_hbm(tokens))


def project_kernel(place, x, a, b, c, d, w_hbm, o0, o1, o2, o3, q4, xs, acc, w_ref, sems):
    t = place[0]
    ctx = place[1]
    copies = [
        pltpu.make_async_copy(w_hbm.at[part], w_ref.at[part], sems.at[part]) for part in range(3)
    ]
    for copy in copies:
        copy.start()
    width = x.shape[1]
    for sub, far in enumerate((c, d)):
        low = sub * SUB
        pieces = [p[low : low + SUB, :] for p in (x, a, b)] + [far[...]]
        squares = jnp.zeros((SUB, 1), f32)
        for piece in pieces:
            wide = piece.astype(f32)
            squares = squares + jnp.sum(wide * wide, axis=1, keepdims=True)
        factor = lax.rsqrt(squares * (1.0 / (4 * width)) + norm_epsilon)
        for distance, piece in zip((0, 3, 1, 2), pieces):
            lane = pl.multiple_of(((t + distance) & 3) * width, 128)
            normed = (piece.astype(f32) * factor).astype(bf16)
            xs[low : low + SUB, pl.ds(lane, width)] = normed

    outs = (o0, o1, o2, o3)
    for part in range(3):
        copies[part].wait()
        acc[part] = jnp.dot(xs[...], w_ref[part], preferred_element_type=f32)

        def column(y):
            if part == 2:
                return y.astype(bf16)
            scale = lax.rsqrt(jnp.mean(y * y, axis=1, keepdims=True) + head_epsilon)
            return (y * scale).astype(bf16)

        for slot, out in enumerate(outs):
            lane = pl.multiple_of(((ctx + slot) & 3) * HD, HD)
            out[part] = column(acc[part, :, pl.ds(lane, HD)])
        z = column(acc[part, :, 4 * HD : 5 * HD])
        if part == 0:
            q4[...] = z
        else:
            for out in outs:
                out[part + 2] = z


def project(place, own, left, right, far_low, far_high, weight, micros):
    width = own.shape[1]
    return pl.pallas_call(
        project_kernel,
        out_shape=(jax.ShapeDtypeStruct((5, HALF, HD), bf16),) * 4
        + (jax.ShapeDtypeStruct((HALF, HD), bf16),),
        in_specs=[pl.BlockSpec(memory_space=pltpu.SMEM)]
        + vmem_specs(5)
        + [pl.BlockSpec(memory_space=pltpu.HBM)],
        out_specs=tuple(vmem_specs(5)),
        scratch_shapes=[
            pltpu.VMEM((HALF, 4 * width), bf16),
            pltpu.VMEM((3, HALF, 5 * HD), f32),
            pltpu.VMEM(weight.shape, bf16),
            pltpu.SemaphoreType.DMA((3,)),
        ],
        compiler_params=params(28),
        cost_estimate=cost(micros),
        name="project",
    )(place, own, left, right, far_low, far_high, in_hbm(weight))


def attend_block(block, count, query, count_of, ks, vs, acc):
    def add_tiles(chunk, base=None):
        scores = [
            jnp.dot(query[at : at + HALF, :], ks[chunk], preferred_element_type=f32)
            for at in (0, HALF)
        ]
        for at, score in zip((0, HALF), scores):
            weights = jnp.exp2(score * EXP2_SCALE)
            if base is not None:
                row = lax.broadcasted_iota(jnp.int32, (HALF, HALF), 0) + (at - base)
                col = lax.broadcasted_iota(jnp.int32, (HALF, HALF), 1)
                weights = jnp.where(col <= row, weights, 0.0)
            acc[at : at + HALF, :] += jnp.dot(
                weights.astype(bf16), vs[chunk], preferred_element_type=f32
            )

    acc[...] = jnp.zeros_like(acc)

    @pl.when(count > 0)
    def _():
        def earlier(chunk, carry):
            @pl.when(count_of(chunk >> 1) > (chunk & 1) * HALF)
            def _():
                add_tiles(chunk)

            return carry

        def same(half, carry):
            @pl.when(count > half * HALF)
            def _():
                add_tiles(2 * block + half, half * HALF)

            return carry

        lax.fori_loop(0, 2 * block, earlier, 0)
        lax.fori_loop(0, 2, same, 0)


def context_of(acc, low):
    total = acc[low : low + HALF, HD:]
    return (acc[low : low + HALF, :HD] / jnp.where(total == 0.0, 1.0, total)).astype(bf16)


def place_keys(chunk, half, count, key, value, ks, vs):
    @pl.when(count > half * HALF)
    def _():
        ks[chunk] = key.T
        rows = lax.broadcasted_iota(jnp.int32, (HALF, HD), 0) + half * HALF
        vs[chunk, :, :HD] = value
        vs[chunk, :, HD:] = jnp.where(rows < count, 1.0, 0.0).astype(bf16)


def attend_main_kernel(first_slot, place, *refs):
    inputs, outs, (qs, ks, vs, cs, acc) = refs[:8], refs[8:10], refs[10:]
    ctx = place[0]

    def count_of(block):
        return place[1 + ((ctx - block) & 3)]

    for s in range(4):
        block = (ctx - s) & 3
        for half in range(2):
            source = inputs[2 * s + half]
            qs[s, half * HALF : (half + 1) * HALF] = source[0]
            place_keys(2 * block + half, half, place[1 + s], source[1], source[2], ks, vs)

    def body(i, carry):
        s = (first_slot + i) & 3
        attend_block((ctx - s) & 3, place[1 + s], qs.at[s], count_of, ks, vs, acc)
        for half in range(2):
            cs[i, half] = context_of(acc, half * HALF)
        return carry

    lax.fori_loop(0, 2, body, 0)
    for i, out in enumerate(outs):
        out[...] = cs[i]


def vmem_specs(count):
    return [pl.BlockSpec(memory_space=pltpu.VMEM)] * count


def attend_main(first_slot, place, inputs):
    return pl.pallas_call(
        functools.partial(attend_main_kernel, first_slot),
        out_shape=(jax.ShapeDtypeStruct((2, HALF, HD), bf16),) * 2,
        in_specs=[pl.BlockSpec(memory_space=pltpu.SMEM)] + vmem_specs(8),
        out_specs=tuple(vmem_specs(2)),
        scratch_shapes=[
            pltpu.VMEM((4, CAP, HD), bf16),
            pltpu.VMEM((8, HD, HALF), bf16),
            pltpu.VMEM((8, HALF, 2 * HD), bf16),
            pltpu.VMEM((2, 2, HALF, HD), bf16),
            pltpu.VMEM((CAP, 2 * HD), f32),
        ],
        compiler_params=params(16),
        cost_estimate=cost(10),
        name="attend_main",
    )(place, *inputs)


def attend_last_kernel(place, *refs):
    inputs, queries, (out, qs, kv, ks, vs, acc, sems) = refs[:8], refs[8:10], refs[10:]
    ctx = place[0]
    copies = [
        pltpu.make_async_copy(source.at[pl.ds(3, 2)], kv.at[i], sems.at[i])
        for i, source in enumerate(inputs)
    ]
    copies += [
        pltpu.make_async_copy(query, qs.at[pl.ds(i * HALF, HALF)], sems.at[8 + i])
        for i, query in enumerate(queries)
    ]
    for copy in copies:
        copy.start()

    def count_of(block):
        return place[1 + ((ctx - block) & 3)]

    for copy in copies:
        copy.wait()
    for s in range(4):

        @pl.when(s <= ctx)
        def _():
            for half in range(2):
                source = kv.at[2 * s + half]
                chunk = (ctx - s) * 2 + half
                place_keys(chunk, half, place[1 + s], source[0], source[1], ks, vs)

    attend_block(ctx, place[1], qs, count_of, ks, vs, acc)
    for half in range(2):
        out[half] = context_of(acc, half * HALF)


def attend_last(place, queries, inputs):
    operands = [in_hbm(a) for a in (*inputs, *queries)]
    return pl.pallas_call(
        attend_last_kernel,
        out_shape=jax.ShapeDtypeStruct((2, HALF, HD), bf16),
        in_specs=[pl.BlockSpec(memory_space=pltpu.SMEM)]
        + [pl.BlockSpec(memory_space=pltpu.HBM)] * 10,
        out_specs=vmem_specs(1)[0],
        scratch_shapes=[
            pltpu.VMEM((CAP, HD), bf16),
            pltpu.VMEM((8, 2, HALF, HD), bf16),
            pltpu.VMEM((8, HD, HALF), bf16),
            pltpu.VMEM((8, HALF, 2 * HD), bf16),
            pltpu.VMEM((CAP, 2 * HD), f32),
            pltpu.SemaphoreType.DMA((10,)),
        ],
        compiler_params=params(16),
        cost_estimate=cost(4),
        name="attend_last",
    )(place, *operands)


def group_term(pieces, weight, cbuf):
    for i, piece in enumerate(pieces):
        cbuf[:, i * HD : (i + 1) * HD] = piece
    term = jnp.dot(cbuf[...], weight, preferred_element_type=f32)
    return term.astype(bf16).astype(f32)


def whole_block(gathered, which, dp):
    places = []
    for share in range(SHARES):
        other = (dp & (SHARES - 1)) ^ share
        places.append((other >> 1, (other & 1) == 1))
    here, there = gathered
    parts = [
        jnp.where(swapped, there[place, which, slot], here[place, which, slot])
        for slot in range(5)
        for place, swapped in places
    ]
    return jnp.concatenate(parts, axis=0)


def add_terms(out, held, cbuf, weight, pieces_of, before):
    held[...] = weight

    def body(half, carry):
        at = pl.ds(pl.multiple_of(half * HALF, HALF), HALF)
        term = group_term(pieces_of(half), held[...], cbuf)
        out[at, :] = term if before is None else before[at, :] + term
        return carry

    lax.fori_loop(0, 2, body, 0)


def pieces_of(first, third, last):
    return lambda half: [first[2 * head + half] for head in range(3)] + [third[half], last[half]]


def own_terms_kernel(place, last, first, third, own, out, cbuf, held):
    starts = [pl.multiple_of(((place[0] + slot) & 3) * HD, HD) for slot in range(4)]
    parts = [own[pl.ds(start, HD), :] for start in starts]
    weight = jnp.concatenate(parts + [own[4 * HD :, :]], axis=0)
    add_terms(out, held, cbuf, weight, pieces_of(first, third, last), None)


def near_terms_kernel(place, before, *refs):
    lasts, firsts, thirds, gathered, (out, cbuf, held) = (
        refs[:2],
        refs[2:4],
        refs[4:6],
        refs[6:8],
        refs[8:],
    )
    for i, (last, first, third) in enumerate(zip(lasts, firsts, thirds)):
        weight = whole_block(gathered, i, place[5])
        add_terms(
            out, held, cbuf, weight, pieces_of(first, third, last), before if i == 0 else out
        )


def terms_call(kernel, name, micros, place, width, operands):
    return pl.pallas_call(
        kernel,
        out_shape=jax.ShapeDtypeStruct((CAP, width), f32),
        in_specs=[pl.BlockSpec(memory_space=pltpu.SMEM)] + vmem_specs(len(operands)),
        out_specs=vmem_specs(1)[0],
        scratch_shapes=[
            pltpu.VMEM((HALF, 5 * HD), bf16),
            pltpu.VMEM((5 * HD, width), bf16),
        ],
        compiler_params=params(12),
        cost_estimate=cost(micros),
        name=name,
    )(place, *operands)


def output_kernel(offs_ref, depth_ref, last, f_low, f_high, third, here, there, near, out, *scratch):
    cbuf, rows, slots = scratch
    step = pl.program_id(0)

    @pl.when(step == 0)
    def _():
        fill_slots(depth_ref, slots)
        rows[CAP:, :] = jnp.zeros((WINDOW, rows.shape[1]), bf16)
        firsts = [f_low[i] for i in range(3)] + [f_high[i] for i in range(3)]
        thirds = [third[0], third[1]]
        weight = whole_block((here, there), 2, offs_ref[depth_ref.shape[0] + 1])
        for half in range(2):
            at = slice(half * HALF, (half + 1) * HALF)
            pieces = [firsts[2 * head + half] for head in range(3)] + [thirds[half], last[half]]
            rows[at, :] = (near[at, :] + group_term(pieces, weight, cbuf)).astype(bf16)

    def body(sub, carry):
        block = step * STEP_BLOCKS + sub
        at = pl.multiple_of(sub * TOK_BLOCK, TOK_BLOCK)

        def run(start, shift_by, window):
            spread = lax.dot_general(
                window_onehot(slots, block, shift_by, window),
                rows[pl.ds(start, window), :],
                (((0,), (0,)), ((), ())),
                preferred_element_type=f32,
            )
            out[pl.ds(at, TOK_BLOCK), :] = spread.astype(bf16)

        by_window(offs_ref, block, run)
        return carry

    lax.fori_loop(0, STEP_BLOCKS, body, 0)


def output_update(offsets, depth_blocks, pieces, gathered, near, length):
    width = near.shape[1]
    blocks = length // TOK_BLOCK
    rows = STEP_BLOCKS * TOK_BLOCK

    operands = (depth_blocks, *pieces, *gathered, near)
    return pl.pallas_call(
        output_kernel,
        out_shape=jax.ShapeDtypeStruct((length, width), bf16),
        grid_spec=pltpu.PrefetchScalarGridSpec(
            num_scalar_prefetch=1,
            grid=(length // rows,),
            in_specs=vmem_specs(len(operands)),
            out_specs=pl.BlockSpec((rows, width), lambda i, o: (i, 0)),
            scratch_shapes=[
                pltpu.VMEM((HALF, 5 * HD), bf16),
                pltpu.VMEM((ROOM, width), bf16),
                pltpu.VMEM((blocks, TOK_BLOCK), jnp.int32),
            ],
        ),
        compiler_params=params(16),
        cost_estimate=cost(8),
        name="output",
    )(offsets, *operands)


def shift(value, axis, distance):
    size = lax.axis_size(axis)
    return lax.ppermute(value, axis, [(i, (i + distance) % size) for i in range(size)])


def swap(value, axis, bit):
    return lax.ppermute(value, axis, [(i, i ^ bit) for i in range(lax.axis_size(axis))])


def after(value, *others):
    return lax.optimization_barrier((value, others))[0]


def ring_near(value):
    return [shift(value, "tensor", 1), shift(value, "tensor", -1)]


def ring_far(near):
    middle = near[0].shape[0] // 2
    return [shift(near[0][:middle], "tensor", 1), shift(near[1][middle:], "tensor", -1)]


def per_device(hidden, depth, qkv_weight, out_weight):
    tokens = hidden[0]
    length, width = tokens.shape
    t = lax.axis_index("tensor")
    ctx = lax.axis_index("ctx")
    depth_blocks = depth.reshape(length // TOK_BLOCK, TOK_BLOCK)
    block_counts = jnp.sum((depth_blocks >= RECURSION).astype(jnp.int32), axis=1)
    ends = jnp.arange(length // TOK_BLOCK + 1)
    offsets = jnp.sum(
        jnp.where(ends[:, None] > ends[None, :-1], block_counts[None, :], 0), axis=1
    ).astype(jnp.int32)
    count = jnp.sum(block_counts).reshape(1)
    place_both = jnp.stack([t, ctx]).astype(jnp.int32)
    weight = jnp.transpose(qkv_weight, (1, 0, 2))

    x0, x1 = compact_rows(tokens, depth_blocks, offsets)


    def column_block(rows, distance):
        start = ((t + distance) & 3) * width
        return lax.dynamic_slice_in_dim(rows, start, width, axis=rows.ndim - 1)

    own_block = column_block(out_weight, 0)
    dp = lax.axis_index("dp")
    shares = out_weight.reshape(5, SHARES, HD // SHARES, out_weight.shape[1])
    shares = lax.dynamic_slice_in_dim(shares, dp & (SHARES - 1), 1, axis=1)[:, 0]
    turned = lax.dynamic_slice_in_dim(jnp.concatenate([shares[:4], shares[:4]]), ctx, 4)
    shares = jnp.concatenate([turned, shares[4:]])

    near0 = ring_near(x0)
    count = after(count, near0)
    others = [shift(count, "ctx", s) for s in (1, 2, 3)]
    far0 = ring_far(near0)
    x1, others = after((x1, others), far0)
    place_ctx = jnp.stack([ctx.astype(jnp.int32), count[0], *[o[0] for o in others], dp.astype(jnp.int32)])
    near1 = ring_near(x1)
    first = project(place_both, x0, *near0, *far0, weight, 9)
    sent0 = [first[0]] + [shift(first[s], "ctx", s) for s in (1, 2, 3)]
    far1 = ring_far(after(near1, first))
    second = project(place_both, x1, *near1, *far1, weight, 9)
    second, shares = after((second, shares), sent0)
    moved = [shift(column_block(shares, d), "tensor", d) for d in (1, 3, 2)]
    gathered = jnp.stack(moved)[None]
    gathered = jnp.concatenate([gathered, swap(gathered, "dp", 2)])
    gathered = (gathered, swap(gathered, "dp", 1))
    sent1 = [second[0]] + [shift(second[s], "ctx", s) for s in (1, 2, 3)]
    arrived = [piece for s in range(4) for piece in (sent0[s], sent1[s])]

    last = attend_last(place_ctx, (first[4], second[4]), arrived)
    lasts = [last] + ring_near(last) + [shift(last, "tensor", 2)]
    to_near, to_far = attend_main(1, after(place_ctx, last), arrived)
    back = [shift(to_near, "ctx", -1), shift(to_far, "ctx", -2)]
    to_right, own = attend_main(3, after(place_ctx, to_near, to_far, lasts), arrived)
    back.append(shift(to_right, "ctx", -3))
    own, lasts, gathered = lax.optimization_barrier((own, lasts, gathered))
    firsts = jnp.concatenate([own, back[0], back[1]])
    near = ring_near(firsts)
    third = after(back[2], near)
    firsts = [firsts] + near + ring_far(near)
    near = ring_near(third)
    thirds = [third] + near + [shift(third, "tensor", 2)]
    operands = (lasts[0], firsts[0], thirds[0], own_block)
    summed = terms_call(own_terms_kernel, "own_terms", 2, place_ctx, width, operands)
    operands = (summed, *lasts[1:3], *firsts[1:3], *thirds[1:3], *gathered)
    summed = terms_call(near_terms_kernel, "near_terms", 4, place_ctx, width, operands)
    pieces = [lasts[3]] + firsts[3:] + thirds[3:]
    update = output_update(
        jnp.concatenate([offsets, dp.reshape(1).astype(jnp.int32)]),
        depth_blocks,
        pieces,
        gathered,
        summed,
        length,
    )
    return update[None]


def solution(mesh):
    placed = (P("dp", "ctx", "tensor"), P("dp", "ctx"), P(None, None, "tensor"), P("tensor", None))
    return jax.shard_map(
        per_device, mesh=mesh, in_specs=placed, out_specs=P("dp", "ctx", "tensor"), check_vma=False
    )
```

```python
import functools
import math

import jax
import jax.numpy as jnp
from jax import lax
from jax.experimental import pallas as pl
from jax.experimental.pallas import tpu as pltpu
from jax.sharding import PartitionSpec as P

HD = 128
RECURSION = 3
CAP = 1024
HALF = CAP // 2
SUB = CAP // 4
TOK_BLOCK = 256
WINDOW = TOK_BLOCK + 16
SMALL = 128
STEP_BLOCKS = 2
SHARES = 4
ROOM = CAP + WINDOW

score_scale = 0.25
norm_epsilon = 1e-05
head_epsilon = 1e-06
EXP2_SCALE = score_scale / math.log(2.0)
MEBI = 1024 * 1024

bf16 = jnp.bfloat16
f32 = jnp.float32


def cost(micros):
    return pl.CostEstimate(flops=int(micros * 1.1e9), bytes_accessed=0, transcendentals=0)


def params(mebibytes):
    return pltpu.CompilerParams(vmem_limit_bytes=mebibytes * MEBI)


def in_hbm(value):
    return pltpu.with_memory_space_constraint(value, pltpu.HBM)


def fill_slots(depth_ref, slots):
    active = depth_ref[...] >= RECURSION
    flags = jnp.where(active, 1.0, 0.0).astype(bf16)
    before = lax.broadcasted_iota(jnp.int32, (TOK_BLOCK, TOK_BLOCK), 0)
    after_it = lax.broadcasted_iota(jnp.int32, (TOK_BLOCK, TOK_BLOCK), 1)
    earlier = jnp.where(before < after_it, 1.0, 0.0).astype(bf16)
    rank = jnp.dot(flags, earlier, preferred_element_type=f32).astype(jnp.int32)
    slots[...] = jnp.where(active, rank, -2 * CAP)


def window_onehot(slots, block, shift_by, window):
    rows = lax.broadcasted_iota(jnp.int32, (window, TOK_BLOCK), 0)
    return jnp.where(rows == slots[pl.ds(block, 1), :] + shift_by, 1.0, 0.0).astype(bf16)


def by_window(offs_ref, block, run):
    low, high = offs_ref[block], offs_ref[block + 1]
    start = pl.multiple_of((low >> 4) << 4, 16)

    @pl.when(high - start <= SMALL)
    def _():
        run(start, low - start, SMALL)

    @pl.when(high - start > SMALL)
    def _():
        run(start, low - start, WINDOW)


def compact_kernel(offs_ref, depth_ref, tok_ref, o0, o1, buf, slots):
    step = pl.program_id(0)

    @pl.when(step == 0)
    def _():
        buf[...] = jnp.zeros_like(buf)
        fill_slots(depth_ref, slots)

    def body(sub, carry):
        block = step * STEP_BLOCKS + sub
        at = pl.multiple_of(sub * TOK_BLOCK, TOK_BLOCK)

        def run(start, shift_by, window):
            picked = jnp.dot(
                window_onehot(slots, block, shift_by, window),
                tok_ref[pl.ds(at, TOK_BLOCK), :],
                preferred_element_type=f32,
            ).astype(bf16)
            buf[pl.ds(start, window), :] = buf[pl.ds(start, window), :] + picked

        by_window(offs_ref, block, run)
        return carry

    lax.fori_loop(0, STEP_BLOCKS, body, 0)

    @pl.when(step == pl.num_programs(0) - 1)
    def _():
        for i, o in enumerate((o0, o1)):
            o[...] = buf[i * HALF : (i + 1) * HALF, :]


def compact_rows(tokens, depth_blocks, offsets):
    length, width = tokens.shape
    blocks = length // TOK_BLOCK
    rows = STEP_BLOCKS * TOK_BLOCK
    return pl.pallas_call(
        compact_kernel,
        out_shape=(jax.ShapeDtypeStruct((HALF, width), bf16),) * 2,
        grid_spec=pltpu.PrefetchScalarGridSpec(
            num_scalar_prefetch=1,
            grid=(length // rows,),
            in_specs=[
                pl.BlockSpec((blocks, TOK_BLOCK), lambda i, o: (0, 0)),
                pl.BlockSpec((rows, width), lambda i, o: (i, 0)),
            ],
            out_specs=(pl.BlockSpec((HALF, width), lambda i, o: (0, 0)),) * 2,
            scratch_shapes=[
                pltpu.VMEM((ROOM, width), bf16),
                pltpu.VMEM((blocks, TOK_BLOCK), jnp.int32),
            ],
        ),
        compiler_params=params(12),
        cost_estimate=cost(8),
        name="compact",
    )(offsets, depth_blocks, in_hbm(tokens))


def project_kernel(place, x, a, b, c, d, w_hbm, o0, o1, o2, o3, q4, xs, acc, w_ref, sems):
    t = place[0]
    ctx = place[1]
    copies = [
        pltpu.make_async_copy(w_hbm.at[part], w_ref.at[part], sems.at[part]) for part in range(3)
    ]
    for copy in copies:
        copy.start()
    width = x.shape[1]
    for sub, far in enumerate((c, d)):
        low = sub * SUB
        pieces = [p[low : low + SUB, :] for p in (x, a, b)] + [far[...]]
        squares = jnp.zeros((SUB, 1), f32)
        for piece in pieces:
            wide = piece.astype(f32)
            squares = squares + jnp.sum(wide * wide, axis=1, keepdims=True)
        factor = lax.rsqrt(squares * (1.0 / (4 * width)) + norm_epsilon)
        for distance, piece in zip((0, 3, 1, 2), pieces):
            lane = pl.multiple_of(((t + distance) & 3) * width, 128)
            normed = (piece.astype(f32) * factor).astype(bf16)
            xs[low : low + SUB, pl.ds(lane, width)] = normed

    outs = (o0, o1, o2, o3)
    for part in range(3):
        copies[part].wait()
        acc[part] = jnp.dot(xs[...], w_ref[part], preferred_element_type=f32)

        def column(y):
            if part == 2:
                return y.astype(bf16)
            scale = lax.rsqrt(jnp.mean(y * y, axis=1, keepdims=True) + head_epsilon)
            return (y * scale).astype(bf16)

        for slot, out in enumerate(outs):
            lane = pl.multiple_of(((ctx + slot) & 3) * HD, HD)
            out[part] = column(acc[part, :, pl.ds(lane, HD)])
        z = column(acc[part, :, 4 * HD : 5 * HD])
        if part == 0:
            q4[...] = z
        else:
            for out in outs:
                out[part + 2] = z


def project(place, own, left, right, far_low, far_high, weight, micros):
    width = own.shape[1]
    return pl.pallas_call(
        project_kernel,
        out_shape=(jax.ShapeDtypeStruct((5, HALF, HD), bf16),) * 4
        + (jax.ShapeDtypeStruct((HALF, HD), bf16),),
        in_specs=[pl.BlockSpec(memory_space=pltpu.SMEM)]
        + vmem_specs(5)
        + [pl.BlockSpec(memory_space=pltpu.HBM)],
        out_specs=tuple(vmem_specs(5)),
        scratch_shapes=[
            pltpu.VMEM((HALF, 4 * width), bf16),
            pltpu.VMEM((3, HALF, 5 * HD), f32),
            pltpu.VMEM(weight.shape, bf16),
            pltpu.SemaphoreType.DMA((3,)),
        ],
        compiler_params=params(28),
        cost_estimate=cost(micros),
        name="project",
    )(place, own, left, right, far_low, far_high, in_hbm(weight))


def attend_block(block, count, query, count_of, ks, vs, acc):
    def add_tiles(chunk, base=None):
        scores = [
            jnp.dot(query[at : at + HALF, :], ks[chunk], preferred_element_type=f32)
            for at in (0, HALF)
        ]
        for at, score in zip((0, HALF), scores):
            weights = jnp.exp2(score * EXP2_SCALE)
            if base is not None:
                row = lax.broadcasted_iota(jnp.int32, (HALF, HALF), 0) + (at - base)
                col = lax.broadcasted_iota(jnp.int32, (HALF, HALF), 1)
                weights = jnp.where(col <= row, weights, 0.0)
            acc[at : at + HALF, :] += jnp.dot(
                weights.astype(bf16), vs[chunk], preferred_element_type=f32
            )

    acc[...] = jnp.zeros_like(acc)

    @pl.when(count > 0)
    def _():
        def earlier(chunk, carry):
            @pl.when(count_of(chunk >> 1) > (chunk & 1) * HALF)
            def _():
                add_tiles(chunk)

            return carry

        def same(half, carry):
            @pl.when(count > half * HALF)
            def _():
                add_tiles(2 * block + half, half * HALF)

            return carry

        lax.fori_loop(0, 2 * block, earlier, 0)
        lax.fori_loop(0, 2, same, 0)


def context_of(acc, low):
    total = acc[low : low + HALF, HD:]
    return (acc[low : low + HALF, :HD] / jnp.where(total == 0.0, 1.0, total)).astype(bf16)


def place_keys(chunk, half, count, key, value, ks, vs):
    @pl.when(count > half * HALF)
    def _():
        ks[chunk] = key.T
        rows = lax.broadcasted_iota(jnp.int32, (HALF, HD), 0) + half * HALF
        vs[chunk, :, :HD] = value
        vs[chunk, :, HD:] = jnp.where(rows < count, 1.0, 0.0).astype(bf16)


def attend_main_kernel(first_slot, place, *refs):
    inputs, outs, (qs, ks, vs, cs, acc) = refs[:8], refs[8:10], refs[10:]
    ctx = place[0]

    def count_of(block):
        return place[1 + ((ctx - block) & 3)]

    for s in range(4):
        block = (ctx - s) & 3
        for half in range(2):
            source = inputs[2 * s + half]
            qs[s, half * HALF : (half + 1) * HALF] = source[0]
            place_keys(2 * block + half, half, place[1 + s], source[1], source[2], ks, vs)

    def body(i, carry):
        s = (first_slot + i) & 3
        attend_block((ctx - s) & 3, place[1 + s], qs.at[s], count_of, ks, vs, acc)
        for half in range(2):
            cs[i, half] = context_of(acc, half * HALF)
        return carry

    lax.fori_loop(0, 2, body, 0)
    for i, out in enumerate(outs):
        out[...] = cs[i]


def vmem_specs(count):
    return [pl.BlockSpec(memory_space=pltpu.VMEM)] * count


def attend_main(first_slot, place, inputs):
    return pl.pallas_call(
        functools.partial(attend_main_kernel, first_slot),
        out_shape=(jax.ShapeDtypeStruct((2, HALF, HD), bf16),) * 2,
        in_specs=[pl.BlockSpec(memory_space=pltpu.SMEM)] + vmem_specs(8),
        out_specs=tuple(vmem_specs(2)),
        scratch_shapes=[
            pltpu.VMEM((4, CAP, HD), bf16),
            pltpu.VMEM((8, HD, HALF), bf16),
            pltpu.VMEM((8, HALF, 2 * HD), bf16),
            pltpu.VMEM((2, 2, HALF, HD), bf16),
            pltpu.VMEM((CAP, 2 * HD), f32),
        ],
        compiler_params=params(16),
        cost_estimate=cost(10),
        name="attend_main",
    )(place, *inputs)


def attend_last_kernel(place, *refs):
    inputs, queries, (out, qs, kv, ks, vs, acc, sems) = refs[:8], refs[8:10], refs[10:]
    ctx = place[0]
    copies = [
        pltpu.make_async_copy(source.at[pl.ds(3, 2)], kv.at[i], sems.at[i])
        for i, source in enumerate(inputs)
    ]
    copies += [
        pltpu.make_async_copy(query, qs.at[pl.ds(i * HALF, HALF)], sems.at[8 + i])
        for i, query in enumerate(queries)
    ]
    for copy in copies:
        copy.start()

    def count_of(block):
        return place[1 + ((ctx - block) & 3)]

    for copy in copies:
        copy.wait()
    for s in range(4):

        @pl.when(s <= ctx)
        def _():
            for half in range(2):
                source = kv.at[2 * s + half]
                chunk = (ctx - s) * 2 + half
                place_keys(chunk, half, place[1 + s], source[0], source[1], ks, vs)

    attend_block(ctx, place[1], qs, count_of, ks, vs, acc)
    for half in range(2):
        out[half] = context_of(acc, half * HALF)


def attend_last(place, queries, inputs):
    operands = [in_hbm(a) for a in (*inputs, *queries)]
    return pl.pallas_call(
        attend_last_kernel,
        out_shape=jax.ShapeDtypeStruct((2, HALF, HD), bf16),
        in_specs=[pl.BlockSpec(memory_space=pltpu.SMEM)]
        + [pl.BlockSpec(memory_space=pltpu.HBM)] * 10,
        out_specs=vmem_specs(1)[0],
        scratch_shapes=[
            pltpu.VMEM((CAP, HD), bf16),
            pltpu.VMEM((8, 2, HALF, HD), bf16),
            pltpu.VMEM((8, HD, HALF), bf16),
            pltpu.VMEM((8, HALF, 2 * HD), bf16),
            pltpu.VMEM((CAP, 2 * HD), f32),
            pltpu.SemaphoreType.DMA((10,)),
        ],
        compiler_params=params(16),
        cost_estimate=cost(4),
        name="attend_last",
    )(place, *operands)


def group_term(pieces, weight, cbuf):
    for i, piece in enumerate(pieces):
        cbuf[:, i * HD : (i + 1) * HD] = piece
    term = jnp.dot(cbuf[...], weight, preferred_element_type=f32)
    return term.astype(bf16).astype(f32)


def whole_block(gathered, which, dp):
    places = []
    for share in range(SHARES):
        other = (dp & (SHARES - 1)) ^ share
        places.append((other >> 1, (other & 1) == 1))
    here, there = gathered
    parts = [
        jnp.where(swapped, there[place, which, slot], here[place, which, slot])
        for slot in range(5)
        for place, swapped in places
    ]
    return jnp.concatenate(parts, axis=0)


def add_terms(out, held, cbuf, weight, pieces_of, before):
    held[...] = weight

    def body(half, carry):
        at = pl.ds(pl.multiple_of(half * HALF, HALF), HALF)
        term = group_term(pieces_of(half), held[...], cbuf)
        out[at, :] = term if before is None else before[at, :] + term
        return carry

    lax.fori_loop(0, 2, body, 0)


def pieces_of(first, third, last):
    return lambda half: [first[2 * head + half] for head in range(3)] + [third[half], last[half]]


def own_terms_kernel(place, last, first, third, own, out, cbuf, held):
    starts = [pl.multiple_of(((place[0] + slot) & 3) * HD, HD) for slot in range(4)]
    parts = [own[pl.ds(start, HD), :] for start in starts]
    weight = jnp.concatenate(parts + [own[4 * HD :, :]], axis=0)
    add_terms(out, held, cbuf, weight, pieces_of(first, third, last), None)


def near_terms_kernel(place, before, *refs):
    lasts, firsts, thirds, gathered, (out, cbuf, held) = (
        refs[:2],
        refs[2:4],
        refs[4:6],
        refs[6:8],
        refs[8:],
    )
    for i, (last, first, third) in enumerate(zip(lasts, firsts, thirds)):
        weight = whole_block(gathered, i, place[5])
        add_terms(
            out, held, cbuf, weight, pieces_of(first, third, last), before if i == 0 else out
        )


def terms_call(kernel, name, micros, place, width, operands):
    return pl.pallas_call(
        kernel,
        out_shape=jax.ShapeDtypeStruct((CAP, width), f32),
        in_specs=[pl.BlockSpec(memory_space=pltpu.SMEM)] + vmem_specs(len(operands)),
        out_specs=vmem_specs(1)[0],
        scratch_shapes=[
            pltpu.VMEM((HALF, 5 * HD), bf16),
            pltpu.VMEM((5 * HD, width), bf16),
        ],
        compiler_params=params(12),
        cost_estimate=cost(micros),
        name=name,
    )(place, *operands)


def output_kernel(offs_ref, depth_ref, last, f_low, f_high, t_low, t_high, here, there, near, out, *scratch):
    cbuf, rows, slots = scratch
    step = pl.program_id(0)

    @pl.when(step == 0)
    def _():
        fill_slots(depth_ref, slots)
        rows[CAP:, :] = jnp.zeros((WINDOW, rows.shape[1]), bf16)
        firsts = [f_low[i] for i in range(3)] + [f_high[i] for i in range(3)]
        thirds = [t_low[0], t_high[0]]
        weight = whole_block((here, there), 2, offs_ref[depth_ref.shape[0] + 1])
        for half in range(2):
            at = slice(half * HALF, (half + 1) * HALF)
            pieces = [firsts[2 * head + half] for head in range(3)] + [thirds[half], last[half]]
            rows[at, :] = (near[at, :] + group_term(pieces, weight, cbuf)).astype(bf16)

    def body(sub, carry):
        block = step * STEP_BLOCKS + sub
        at = pl.multiple_of(sub * TOK_BLOCK, TOK_BLOCK)

        def run(start, shift_by, window):
            spread = lax.dot_general(
                window_onehot(slots, block, shift_by, window),
                rows[pl.ds(start, window), :],
                (((0,), (0,)), ((), ())),
                preferred_element_type=f32,
            )
            out[pl.ds(at, TOK_BLOCK), :] = spread.astype(bf16)

        by_window(offs_ref, block, run)
        return carry

    lax.fori_loop(0, STEP_BLOCKS, body, 0)


def output_update(offsets, depth_blocks, pieces, gathered, near, length):
    width = near.shape[1]
    blocks = length // TOK_BLOCK
    rows = STEP_BLOCKS * TOK_BLOCK

    operands = (depth_blocks, *pieces, *gathered, near)
    return pl.pallas_call(
        output_kernel,
        out_shape=jax.ShapeDtypeStruct((length, width), bf16),
        grid_spec=pltpu.PrefetchScalarGridSpec(
            num_scalar_prefetch=1,
            grid=(length // rows,),
            in_specs=vmem_specs(len(operands)),
            out_specs=pl.BlockSpec((rows, width), lambda i, o: (i, 0)),
            scratch_shapes=[
                pltpu.VMEM((HALF, 5 * HD), bf16),
                pltpu.VMEM((ROOM, width), bf16),
                pltpu.VMEM((blocks, TOK_BLOCK), jnp.int32),
            ],
        ),
        compiler_params=params(16),
        cost_estimate=cost(8),
        name="output",
    )(offsets, *operands)


def shift(value, axis, distance):
    size = lax.axis_size(axis)
    return lax.ppermute(value, axis, [(i, (i + distance) % size) for i in range(size)])


def swap(value, axis, bit):
    return lax.ppermute(value, axis, [(i, i ^ bit) for i in range(lax.axis_size(axis))])


def after(value, *others):
    return lax.optimization_barrier((value, others))[0]


def ring_near(value):
    return [shift(value, "tensor", 1), shift(value, "tensor", -1)]


def ring_far(near):
    middle = near[0].shape[0] // 2
    return [shift(near[0][:middle], "tensor", 1), shift(near[1][middle:], "tensor", -1)]


def per_device(hidden, depth, qkv_weight, out_weight):
    tokens = hidden[0]
    length, width = tokens.shape
    t = lax.axis_index("tensor")
    ctx = lax.axis_index("ctx")
    depth_blocks = depth.reshape(length // TOK_BLOCK, TOK_BLOCK)
    block_counts = jnp.sum((depth_blocks >= RECURSION).astype(jnp.int32), axis=1)
    ends = jnp.arange(length // TOK_BLOCK + 1)
    offsets = jnp.sum(
        jnp.where(ends[:, None] > ends[None, :-1], block_counts[None, :], 0), axis=1
    ).astype(jnp.int32)
    count = jnp.sum(block_counts).reshape(1)
    place_both = jnp.stack([t, ctx]).astype(jnp.int32)
    weight = jnp.transpose(qkv_weight, (1, 0, 2))

    x0, x1 = compact_rows(tokens, depth_blocks, offsets)


    def column_block(rows, distance):
        start = ((t + distance) & 3) * width
        return lax.dynamic_slice_in_dim(rows, start, width, axis=rows.ndim - 1)

    own_block = column_block(out_weight, 0)
    dp = lax.axis_index("dp")
    shares = out_weight.reshape(5, SHARES, HD // SHARES, out_weight.shape[1])
    shares = lax.dynamic_slice_in_dim(shares, dp & (SHARES - 1), 1, axis=1)[:, 0]
    turned = lax.dynamic_slice_in_dim(jnp.concatenate([shares[:4], shares[:4]]), ctx, 4)
    shares = jnp.concatenate([turned, shares[4:]])

    near0 = ring_near(x0)
    count = after(count, near0)
    others = [shift(count, "ctx", s) for s in (1, 2, 3)]
    far0 = ring_far(near0)
    x1, others = after((x1, others), far0)
    place_ctx = jnp.stack([ctx.astype(jnp.int32), count[0], *[o[0] for o in others], dp.astype(jnp.int32)])
    near1 = ring_near(x1)
    first = project(place_both, x0, *near0, *far0, weight, 9)
    sent0 = [first[0]] + [shift(first[s], "ctx", s) for s in (1, 2, 3)]
    far1 = ring_far(after(near1, first))
    second = project(place_both, x1, *near1, *far1, weight, 9)
    second, shares = after((second, shares), sent0)
    moved = [shift(column_block(shares, d), "tensor", d) for d in (1, 3, 2)]
    gathered = jnp.stack(moved)[None]
    gathered = jnp.concatenate([gathered, swap(gathered, "dp", 2)])
    gathered = (gathered, swap(gathered, "dp", 1))
    sent1 = [second[0]] + [shift(second[s], "ctx", s) for s in (1, 2, 3)]
    arrived = [piece for s in range(4) for piece in (sent0[s], sent1[s])]

    last = attend_last(place_ctx, (first[4], second[4]), arrived)
    lasts = [last] + ring_near(last) + [shift(last, "tensor", 2)]
    to_near, to_far = attend_main(1, after(place_ctx, last), arrived)
    back = [shift(to_near, "ctx", -1), shift(to_far, "ctx", -2)]
    to_right, own = attend_main(3, after(place_ctx, to_near, to_far, lasts), arrived)
    back.append(shift(to_right, "ctx", -3))
    own, lasts, gathered = lax.optimization_barrier((own, lasts, gathered))
    firsts = jnp.concatenate([own, back[0], back[1]])
    near = ring_near(firsts)
    third = after(back[2], near)
    firsts = [firsts] + near + ring_far(near)
    near = ring_near(third)
    thirds = [third] + near + ring_far(near)
    operands = (lasts[0], firsts[0], thirds[0], own_block)
    summed = terms_call(own_terms_kernel, "own_terms", 2, place_ctx, width, operands)
    operands = (summed, *lasts[1:3], *firsts[1:3], *thirds[1:3], *gathered)
    summed = terms_call(near_terms_kernel, "near_terms", 4, place_ctx, width, operands)
    pieces = [lasts[3]] + firsts[3:] + thirds[3:]
    update = output_update(
        jnp.concatenate([offsets, dp.reshape(1).astype(jnp.int32)]),
        depth_blocks,
        pieces,
        gathered,
        summed,
        length,
    )
    return update[None]


def solution(mesh):
    placed = (P("dp", "ctx", "tensor"), P("dp", "ctx"), P(None, None, "tensor"), P("tensor", None))
    return jax.shard_map(
        per_device, mesh=mesh, in_specs=placed, out_specs=P("dp", "ctx", "tensor"), check_vma=False
    )
```
